32 devices in a mesh: band: 8 (over z, y), mp: 4 (over x, core).
Axes of the slice: x: 2, y: 2, z: 4, core: 2. Of those that a mesh axis runs over, the one named last changes fastest.
Arguments:
- node_adjoint: bfloat16 [8192, 512], P('band'), may hold values from -6 to 6
- band_map: int32 [8, 1024], P('band'), may hold values from 0 to 1023, each once within a row
- latents: bfloat16 [8192, 512], P('band'), may hold values from -20 to 20
- observations: bfloat16 [4096, 512], P('band'), may hold values from -6 to 6
- route_band: int32 [4096, 1], P('band'), may hold values from 0 to 7; in each aligned block of 512 rows (0 to 511, 512 to 1023, ...) at most 128 rows name the same one
- route_cell: int32 [4096], P('band'), may hold values from 0 to 1023
- block_mask: int32 [64, 8], P('band'), may hold values 0 or 1
- w_query: bfloat16 [512, 512], P(None, 'mp'), may hold values from -2 to 2
- w_key: bfloat16 [512, 512], P(None, 'mp'), may hold values from -2 to 2
- w_value: bfloat16 [512, 512], P(None, 'mp'), may hold values from -0.25 to 0.25
- w_out: bfloat16 [512, 512], P('mp'), may hold values from -0.25 to 0.25
Outputs:
- node_grad: bfloat16 [8192, 512], P('band', 'mp')
- observation_grad: bfloat16 [4096, 512], P('band', 'mp')
The draws below stay inside these ranges and needn't reach their ends.
Inputs may be any that keep to these rules, and one draw needn't show every extreme that they name: Row q places the 1024 nodes of band q in the processor's partitions: node n of band q is row q * 128 + band_map[q, n] % 128 of partition band_map[q, n] // 128; each row holds every value once. `route_band`: within the rows of one device no band is named by more than 128 rows, a bound that some block reaches.
All inputs are finite; a program needn't handle non-finite values. No bound on the sum of `block_mask` on one device may be relied on, other than what follows from the above.
Results may differ from the reference program's by a relative error of at most 0.012.
The reference program's roundings to bfloat16 on the way count: a program that leaves them out, or rounds other values in their place, can miss the bound.
Values may be sent and summed in bfloat16 or wider, within the bound.
A program may use at most 64 MiB of HBM per device.

```python
import math
import jax
import jax.numpy as jnp
import numpy as np
from jax import lax

D = 512
HEADS = 16
HEAD_DIM = 32
BLOCK = 128
NODES_PER_BAND = 1024
OBS_DEV = 512
CAP = 128
KEYS = 1024
GROUP = 128
NODE_BLOCKS = 8
NODES = 8192
OBS = 4096
N_BAND = 8
N_MP = 4


def drawn_weight(key, salt):
    noise = jax.random.normal(jax.random.fold_in(key, salt), (D, D), jnp.float32)
    noise = jnp.clip(noise, -4.0, 4.0) / jnp.sqrt(jnp.float32(D))
    return noise.astype(jnp.bfloat16)


def draw_w_query(key, part):
    return drawn_weight(key, 3)


def draw_w_key(key, part):
    return drawn_weight(key, 5)


def draw_latents(key, part):
    base = jnp.clip(jax.random.normal(jax.random.fold_in(key, 2), (NODES, D), jnp.float32), -4.0, 4.0)
    return base.astype(jnp.bfloat16)


def place_ends(drawn, stream_key, smallest, high):
    index_at = [jax.random.randint(jax.random.fold_in(stream_key, axis), (), 0, length) for axis, length in enumerate(drawn.shape)]
    widest = drawn.shape.index(max(drawn.shape))
    beside = index_at[:widest] + [(index_at[widest] + 1) % drawn.shape[widest]] + index_at[widest + 1:]
    return drawn.at[tuple(index_at)].set(smallest).at[tuple(beside)].set(high)


def block_scale(own_key, shape, shards, smallest, high):
    level = 1.0
    for position, blocks in shards:
        heights = jax.random.uniform(jax.random.fold_in(jax.random.fold_in(own_key, 6), position), (blocks,), jnp.float32, smallest / len(shards), high / len(shards))
        level = level * jnp.repeat(jnp.exp(heights), shape[position] // blocks).reshape((-1,) + (1,) * (len(shape) - 1 - position))
    return level


def assign_block(rng, own, number, rows, number_of, top, reach, lean):
    order = jax.random.permutation(rng, number_of)
    crowded, ordinary = load_shares(number_of, rows * top, reach, lean, True), load_shares(number_of, rows * top, reach, lean, False)
    places = jnp.arange(number_of)

    def named(sizes, turn):
        used = int((sizes > 0).sum())
        fixed = max(1, used // 4)
        shifted = fixed + (places - fixed + turn * (used - fixed)) % max(1, number_of - fixed)
        return jnp.zeros((number_of,), jnp.int32).at[order[jnp.where(places < fixed, places, shifted)]].set(jnp.asarray(sizes, jnp.int32))

    sizes = jnp.where(number % 4 == 0, named(crowded, number // 4), named(ordinary, number - number // 4 - 1))
    mixed = jax.random.permutation(jax.random.fold_in(own, 3), number_of)
    giver, sink = mixed[0:number_of // 2 * 2:2], mixed[1:number_of // 2 * 2:2]
    slack = jnp.minimum(sizes[giver] - 1, reach - sizes[sink]) // 2
    slack = jnp.where((giver == order[0]) | (sink == order[0]) | (sizes[sink] == 0), 0, jnp.maximum(slack, 0))
    shifted = jax.random.randint(jax.random.fold_in(own, 4), (number_of // 2,), 0, 1 << 20) % (slack + 1)
    sizes = sizes.at[giver].add(-shifted).at[sink].add(shifted)
    labels = jnp.searchsorted(jnp.cumsum(sizes), jnp.arange(rows * top), side="right").astype(jnp.int32)
    listing = labels.reshape(top, rows).T
    listing = listing[jax.random.permutation(jax.random.fold_in(own, 1), rows)]
    turn = jax.random.randint(jax.random.fold_in(own, 2), (rows, 1), 0, top)
    return jnp.take_along_axis(listing, (jnp.arange(top)[None, :] + turn) % top, axis=1)


def load_shares(number_of, total, limit, slope, full):
    loads = [(1 << 20) // math.isqrt(standing ** slope) + 1 for standing in range(1, number_of + 1)]
    largest = limit if full else min(limit, max(-(-total // number_of), total * loads[0] // sum(loads)))
    least = 1 if total - largest >= number_of - 1 else 0
    holding, surplus = [largest] + [least] * (number_of - 1), total - largest - least * (number_of - 1)
    while surplus > 0:
        movable = [i for i in range(1, number_of) if holding[i] < largest] or [i for i in range(1, number_of) if holding[i] < limit]
        mass, remaining = sum([loads[i] for i in movable]), surplus
        for i in movable:
            addition = min(limit - holding[i], max(1, remaining * loads[i] // mass), surplus)
            holding[i] = holding[i] + addition
            surplus = surplus - addition
    return np.array(holding)


def normal_values(stream_key, extent, width, bound, shards=(), kind=jnp.bfloat16):
    values = width * jax.random.normal(stream_key, extent, jnp.float32)
    if shards:
        values = values * block_scale(stream_key, extent, shards, -0.22, 0.18)
    return jnp.clip(values, -bound, bound).astype(kind)


def setup_inputs(seed: int = 0) -> dict:
    keys = jax.random.split(jax.random.key(seed), 12)
    node_adjoint = normal_values(keys[0], (NODES, D), 1.0, 6.0, ((0, 8),))
    band_map = jax.vmap(lambda own: jax.random.permutation(own, NODES_PER_BAND))(jax.random.split(keys[1], N_BAND)).reshape((N_BAND, NODES_PER_BAND)).astype(jnp.int32)
    latents = draw_latents(jax.random.fold_in(keys[11], 71), 0)
    observations = normal_values(keys[3], (OBS, D), 1.0, 6.0, ((0, 8),))
    route_band_keys = jax.random.split(jax.random.fold_in(keys[4], 1), OBS // OBS_DEV)
    route_band_turns = jax.random.permutation(jax.random.fold_in(keys[4], 3), OBS // OBS_DEV)
    route_band = jax.vmap(lambda own, number: assign_block(jax.random.fold_in(keys[4], 2), own, number, OBS_DEV, N_BAND, 1, CAP, 2))(route_band_keys, route_band_turns).reshape((OBS, 1))
    route_cell = place_ends(jax.random.randint(keys[5], (OBS,), 0, NODES_PER_BAND), jax.random.fold_in(keys[5], 1), 0, NODES_PER_BAND - 1).astype(jnp.int32)
    block_mask = place_ends((jax.random.randint(keys[6], (N_BAND * NODE_BLOCKS, NODE_BLOCKS), 0, 2) < 1).astype(jnp.int32), jax.random.fold_in(keys[6], 1), 0, 1)
    w_query = draw_w_query(jax.random.fold_in(keys[11], 71), 0)
    w_key = draw_w_key(jax.random.fold_in(keys[11], 71), 0)
    w_value = normal_values(keys[9], (D, D), D ** -0.5, 0.25, ((1, 4),))
    w_out = normal_values(keys[10], (D, D), D ** -0.5, 0.25, ((0, 4),))
    return dict(node_adjoint=node_adjoint, band_map=band_map, latents=latents, observations=observations, route_band=route_band, route_cell=route_cell, block_mask=block_mask, w_query=w_query, w_key=w_key, w_value=w_value, w_out=w_out)


def dot_wide(left, right):
    return jnp.dot(left, right, preferred_element_type=jnp.float32)

def broaden_precision(value):
    return lax.optimization_barrier(value).astype(jnp.float32)

def separate_heads(value, row_total):
    return broaden_precision(value).reshape(row_total, HEADS, HEAD_DIM)

def band_grads(latent_rows, adjoint_rows, mask_rows, pair_band, cell_band, w_query, w_key, w_value, w_out):
    score_factor_scale = 1.0 / math.sqrt(HEAD_DIM)
    queries = (dot_wide(latent_rows, w_query) * score_factor_scale).astype(jnp.bfloat16)
    self_pair_key = dot_wide(latent_rows, w_key).astype(jnp.bfloat16)
    self_value = dot_wide(latent_rows, w_value).astype(jnp.bfloat16)
    grad_out = dot_wide(adjoint_rows, jnp.transpose(w_out)).astype(jnp.bfloat16)
    key_hot = ((cell_band // BLOCK)[:, None] == jnp.arange(NODE_BLOCKS, dtype=jnp.int32)[None, :]).astype(jnp.float32)
    node_mask = jnp.repeat(mask_rows.astype(jnp.float32), BLOCK, axis=0)
    allowed = (dot_wide(node_mask, jnp.transpose(key_hot)) > 0.5)[None]
    query_head_split = separate_heads(queries, NODES_PER_BAND)
    self_key_head_split = separate_heads(self_pair_key, NODES_PER_BAND)
    svalue_heads = separate_heads(self_value, NODES_PER_BAND)
    grad_heads = separate_heads(grad_out, NODES_PER_BAND)
    key_head_split = separate_heads(pair_band[:, :D], KEYS)
    value_heads = separate_heads(pair_band[:, D:], KEYS)
    scores = jnp.einsum('nhd,khd->hnk', query_head_split, key_head_split)
    self_score = jnp.transpose(lax.optimization_barrier(jnp.sum(query_head_split * self_key_head_split, axis=2)))
    highest = jnp.maximum(lax.optimization_barrier(jnp.max(jnp.where(allowed, scores, -jnp.inf), axis=2)), self_score)
    weights = jnp.where(allowed, jnp.exp(scores - highest[:, :, None]), 0.0)
    own_weight = jnp.exp(self_score - highest)
    normaliser = lax.optimization_barrier(jnp.sum(weights, axis=2)) + own_weight
    probabilities = weights / normaliser[:, :, None]
    own_prob = own_weight / normaliser
    probabilities_low = broaden_precision(probabilities.astype(jnp.bfloat16))
    dprobs = jnp.einsum('nhd,khd->hnk', grad_heads, value_heads)
    own_dprob = jnp.transpose(lax.optimization_barrier(jnp.sum(grad_heads * svalue_heads, axis=2)))
    centre = lax.optimization_barrier(jnp.sum(probabilities * dprobs, axis=2)) + own_prob * own_dprob
    dscore = probabilities * (dprobs - centre[:, :, None])
    own_dscore = own_prob * (own_dprob - centre)
    score_gradient_narrow = broaden_precision(dscore.astype(jnp.bfloat16))
    self_score_gradient_rows = jnp.transpose(own_dscore)[:, :, None]
    own_prob_rows = jnp.transpose(own_prob)[:, :, None]
    query_gradient = (jnp.einsum('emc,cez->mez', score_gradient_narrow, key_head_split) + self_score_gradient_rows * self_key_head_split) * score_factor_scale
    query_gradient = query_gradient.astype(jnp.bfloat16).reshape(NODES_PER_BAND, D)
    dself_key = (self_score_gradient_rows * query_head_split).astype(jnp.bfloat16).reshape(NODES_PER_BAND, D)
    dself_value = (own_prob_rows * grad_heads).astype(jnp.bfloat16).reshape(NODES_PER_BAND, D)
    dkey = jnp.einsum('hnk,nhd->khd', score_gradient_narrow, query_head_split).astype(jnp.bfloat16).reshape(KEYS, D)
    dvalue = jnp.einsum('hnk,nhd->khd', probabilities_low, grad_heads).astype(jnp.bfloat16).reshape(KEYS, D)
    stride = D // N_MP
    node_sum = jnp.zeros((NODES_PER_BAND, D), jnp.float32)
    for group_index in range(N_MP):
        column_start = group_index * stride
        column_stop = column_start + stride
        group_term = dot_wide(query_gradient[:, column_start:column_stop], jnp.transpose(w_query[:, column_start:column_stop]))
        group_term = group_term + dot_wide(dself_key[:, column_start:column_stop], jnp.transpose(w_key[:, column_start:column_stop]))
        group_term = group_term + dot_wide(dself_value[:, column_start:column_stop], jnp.transpose(w_value[:, column_start:column_stop]))
        node_sum = node_sum + broaden_precision(group_term.astype(jnp.bfloat16))
    node_grad = (adjoint_rows.astype(jnp.float32) + node_sum).astype(jnp.bfloat16)
    return (node_grad, jnp.concatenate([dkey, dvalue], axis=1))

def reference(node_adjoint, band_map, latents, observations, route_band, route_cell, block_mask, w_query, w_key, w_value, w_out):
    band_index = jnp.arange(N_BAND, dtype=jnp.int32)[:, None]
    source_row = band_map // GROUP * NODES_PER_BAND + band_index * GROUP + band_map % GROUP
    adjoint = jnp.take(node_adjoint, source_row.reshape(-1).astype(jnp.int32), axis=0)
    target = route_band[:, 0]
    onehot = (target[:, None] == jnp.arange(N_BAND, dtype=jnp.int32)[None, :]).astype(jnp.int32)
    onehot = onehot.reshape(N_BAND, OBS_DEV, N_BAND)
    earlier = jnp.cumsum(onehot, axis=1) - onehot
    rank_within = lax.optimization_barrier(jnp.sum(earlier * onehot, axis=2)).reshape(-1).astype(jnp.int32)
    source = jnp.arange(OBS, dtype=jnp.int32) // OBS_DEV
    slot_index = source * CAP + rank_within
    gather_index = jnp.full((N_BAND, KEYS), OBS, jnp.int32).at[target, slot_index].set(jnp.arange(OBS, dtype=jnp.int32))
    cell_padded = jnp.concatenate([route_cell, jnp.full((1,), -1, jnp.int32)])
    slot_cells = jnp.take(cell_padded, gather_index, axis=0)
    pair_rows = jnp.concatenate([dot_wide(observations, w_key).astype(jnp.bfloat16), dot_wide(observations, w_value).astype(jnp.bfloat16)], axis=1)
    pair_padded = jnp.concatenate([pair_rows, jnp.zeros((1, 2 * D), jnp.bfloat16)], axis=0)
    slot_pairs = jnp.take(pair_padded, gather_index, axis=0)

    def one_band(band_items):
        latent_rows, adjoint_rows, mask_rows, pair_band, cell_band = band_items
        return band_grads(latent_rows, adjoint_rows, mask_rows, pair_band, cell_band, w_query, w_key, w_value, w_out)
    node_grad, pair_grads = lax.map(one_band, (latents.reshape(N_BAND, NODES_PER_BAND, D), adjoint.reshape(N_BAND, NODES_PER_BAND, D), block_mask.reshape(N_BAND, NODE_BLOCKS, NODE_BLOCKS), slot_pairs, slot_cells))
    own_pairs = jnp.take(pair_grads.reshape(N_BAND * KEYS, 2 * D), (target * KEYS + slot_index).astype(jnp.int32), axis=0)
    stride = D // N_MP
    observed_sum = jnp.zeros((OBS, D), jnp.float32)
    for group_index in range(N_MP):
        column_start = group_index * stride
        column_stop = column_start + stride
        group_term = dot_wide(own_pairs[:, column_start:column_stop], jnp.transpose(w_key[:, column_start:column_stop]))
        group_term = group_term + dot_wide(own_pairs[:, D + column_start:D + column_stop], jnp.transpose(w_value[:, column_start:column_stop]))
        observed_sum = observed_sum + broaden_precision(group_term.astype(jnp.bfloat16))
    return (node_grad.reshape(NODES, D), observed_sum.astype(jnp.bfloat16))
```

```python
import functools
import math

import jax
import jax.numpy as jnp
from jax import lax
from jax.experimental import pallas as pl
from jax.experimental.pallas import tpu as pltpu
from jax.sharding import PartitionSpec as P

HEAD_DIM = 32
BLOCK = 128


def dot_wide(left, right):
    return jnp.dot(left, right, preferred_element_type=jnp.float32)


def dot_transposed(left, right):
    return lax.dot_general(
        left, right, (((1,), (1,)), ((), ())), preferred_element_type=jnp.float32
    )


def broaden_precision(value):
    return lax.optimization_barrier(value).astype(jnp.float32)


def send_slots(route_band, band_count, capacity):
    target = route_band[:, 0]
    onehot = (target[:, None] == jnp.arange(band_count, dtype=jnp.int32)[None, :]).astype(jnp.int32)
    earlier = jnp.cumsum(onehot, axis=0) - onehot
    rank_within = jnp.sum(earlier * onehot, axis=1)
    return target * capacity + rank_within


def on_device_plain(
    node_adjoint,
    band_map,
    latents,
    observations,
    route_band,
    route_cell,
    block_mask,
    w_query,
    w_key,
    w_value,
    w_out,
):
    band_count = lax.axis_size("band")
    node_count = latents.shape[0]
    column_count = w_query.shape[1]
    head_count = column_count // HEAD_DIM
    observed_rows = observations.shape[0]
    capacity = 2 * observed_rows // band_count
    slot_count = capacity * band_count
    block_count = block_mask.shape[1]
    model_index = lax.axis_index("mp")
    score_factor_scale = 1.0 / math.sqrt(HEAD_DIM)
    w_pair = jnp.concatenate([w_key, w_value], axis=1)
    arrival = band_map[0]
    received = lax.all_to_all(node_adjoint, "band", split_axis=0, concat_axis=0, tiled=True)
    adjoint = jnp.take(received, arrival, axis=0)
    adjoint_part = lax.dynamic_slice_in_dim(adjoint, model_index * column_count, column_count, 1)
    target_slot = send_slots(route_band, band_count, capacity)
    cell_send = jnp.full((slot_count,), -1, jnp.int32).at[target_slot].set(route_cell)
    own_rows = lax.dynamic_slice_in_dim(observations, model_index * column_count, column_count, 1)
    row_send = jnp.zeros((slot_count, column_count), jnp.bfloat16).at[target_slot].set(own_rows)
    row_arrived, slot_cells = (
        lax.all_to_all(row_send, "band", split_axis=0, concat_axis=0, tiled=True),
        lax.all_to_all(cell_send, "band", split_axis=0, concat_axis=0, tiled=True),
    )
    full_rows = lax.all_gather(row_arrived, "mp", axis=1, tiled=True)
    key_pairs = dot_wide(full_rows, w_pair).astype(jnp.bfloat16)
    key_head_split = key_pairs[:, :column_count].reshape(slot_count, head_count, HEAD_DIM)
    value_heads = key_pairs[:, column_count:].reshape(slot_count, head_count, HEAD_DIM)
    key_hot = (
        (slot_cells // BLOCK)[:, None] == jnp.arange(block_count, dtype=jnp.int32)[None, :]
    ).astype(jnp.bfloat16)
    node_mask = jnp.repeat(block_mask, BLOCK, axis=0).astype(jnp.bfloat16)
    queries = (dot_wide(latents, w_query) * score_factor_scale).astype(jnp.bfloat16)
    self_pair = dot_wide(latents, w_pair).astype(jnp.bfloat16)
    self_pair_key = self_pair[:, :column_count]
    self_value = self_pair[:, column_count:]
    grad_out = dot_transposed(adjoint, w_out).astype(jnp.bfloat16)
    block_rows = min(512, node_count)
    block_total = node_count // block_rows

    def split_blocks(value):
        return value.reshape(block_total, block_rows, head_count, HEAD_DIM)

    stacked = (
        split_blocks(queries),
        split_blocks(self_pair_key),
        split_blocks(self_value),
        split_blocks(grad_out),
        node_mask.reshape(block_total, block_rows, block_count),
    )

    def attend(running, block_entries):
        key_grad, value_grad = running
        query_tile, self_key_tile, self_value_tile, gradient_block, block_mask_tile = block_entries
        scores = jnp.einsum(
            "qhd,khd->hqk", query_tile, key_head_split, preferred_element_type=jnp.float32
        )
        allowed = (dot_transposed(block_mask_tile, key_hot) > 0.5)[None]
        query_widened = broaden_precision(query_tile)
        grad_wide = broaden_precision(gradient_block)
        self_key_widened = broaden_precision(self_key_tile)
        self_score = jnp.transpose(jnp.sum(query_widened * self_key_widened, axis=2))
        highest = jnp.maximum(jnp.max(jnp.where(allowed, scores, -jnp.inf), axis=2), self_score)
        weights = jnp.where(allowed, jnp.exp(scores - highest[:, :, None]), 0.0)
        own_weight = jnp.exp(self_score - highest)
        normaliser = jnp.sum(weights, axis=2) + own_weight
        probabilities = weights / normaliser[:, :, None]
        own_prob = own_weight / normaliser
        probabilities_low = probabilities.astype(jnp.bfloat16)
        dprobs = jnp.einsum(
            "qhd,khd->hqk", gradient_block, value_heads, preferred_element_type=jnp.float32
        )
        own_dprob = jnp.transpose(jnp.sum(grad_wide * broaden_precision(self_value_tile), axis=2))
        centre = jnp.sum(probabilities * dprobs, axis=2) + own_prob * own_dprob
        dscore = probabilities * (dprobs - centre[:, :, None])
        own_dscore = own_prob * (own_dprob - centre)
        score_gradient_narrow = dscore.astype(jnp.bfloat16)
        self_score_gradient_rows = jnp.transpose(own_dscore)[:, :, None]
        own_prob_rows = jnp.transpose(own_prob)[:, :, None]
        query_gradient = jnp.einsum(
            "hqk,khd->qhd",
            score_gradient_narrow,
            key_head_split,
            preferred_element_type=jnp.float32,
        )
        query_gradient = (
            (query_gradient + self_score_gradient_rows * self_key_widened) * score_factor_scale
        ).astype(jnp.bfloat16)
        dself_key = (self_score_gradient_rows * query_widened).astype(jnp.bfloat16)
        dself_value = (own_prob_rows * grad_wide).astype(jnp.bfloat16)
        key_grad = key_grad + jnp.einsum(
            "hqk,qhd->khd", score_gradient_narrow, query_tile, preferred_element_type=jnp.float32
        )
        value_grad = value_grad + jnp.einsum(
            "hqk,qhd->khd", probabilities_low, gradient_block, preferred_element_type=jnp.float32
        )
        flat_shape = (block_rows, column_count)
        node_pieces = jnp.concatenate(
            [
                query_gradient.reshape(flat_shape),
                dself_key.reshape(flat_shape),
                dself_value.reshape(flat_shape),
            ],
            axis=1,
        )
        return ((key_grad, value_grad), node_pieces)

    zero_grads = jnp.zeros((slot_count, head_count, HEAD_DIM), jnp.float32)
    (key_grad, value_grad), node_pieces = lax.scan(attend, (zero_grads, zero_grads), stacked)
    node_pieces = node_pieces.reshape(node_count, 3 * column_count)
    w_triple = jnp.concatenate([w_query, w_key, w_value], axis=1)
    node_term = dot_transposed(node_pieces, w_triple)
    node_sum = lax.psum_scatter(
        node_term.astype(jnp.bfloat16), "mp", scatter_dimension=1, tiled=True
    ).astype(jnp.float32)
    node_grad = (adjoint_part.astype(jnp.float32) + node_sum).astype(jnp.bfloat16)
    grad_pairs = jnp.concatenate(
        [
            key_grad.astype(jnp.bfloat16).reshape(slot_count, column_count),
            value_grad.astype(jnp.bfloat16).reshape(slot_count, column_count),
        ],
        axis=1,
    )
    slot_term = dot_transposed(grad_pairs, w_pair)
    slot_sum = lax.psum_scatter(
        slot_term.astype(jnp.bfloat16), "mp", scatter_dimension=1, tiled=True
    )
    returned = lax.all_to_all(slot_sum, "band", split_axis=0, concat_axis=0, tiled=True)
    observation_grad = jnp.take(returned, target_slot, axis=0)
    return (node_grad, observation_grad)


TILE = 256
HEADS_PER_PASS = 2
MESH = pl.DeviceIdType.MESH


def dot_first(left, right):
    return lax.dot_general(
        left, right, (((0,), (0,)), ((), ())), preferred_element_type=jnp.float32
    )


def column_of(row, rows=128):
    wide = jnp.transpose(jnp.broadcast_to(row.astype(jnp.float32), (rows, row.shape[1])))
    return wide[:, :1].astype(jnp.int32)


def encoder_kernel(
    bands,
    models,
    adjoint_ref,
    map_ref,
    latents_ref,
    observed_ref,
    band_ref,
    cell_ref,
    mask_ref,
    wq_ref,
    wk_ref,
    wv_ref,
    wo_ref,
    node_out,
    observed_out,
    key_send,
    value_send,
    hot_send,
    grad_send,
    key_got,
    value_got,
    hot_got,
    grad_got,
    adj_got,
    query_s,
    query_t,
    skey_s,
    svalue_s,
    grad_s,
    grad_t,
    key_heads,
    value_heads,
    bias_s,
    dkey_t,
    dvalue_t,
    dquery_s,
    dscore_s,
    prob_s,
    back_send,
    back_got,
    node_send,
    node_got,
    obs_send,
    obs_got,
    in_send,
    in_recv,
    back_send_sem,
    back_recv_sem,
    node_send_sem,
    node_recv_sem,
    obs_send_sem,
    obs_recv_sem,
):
    me = lax.axis_index("band")
    mine = lax.axis_index("mp")
    nodes = latents_ref.shape[0]
    columns = wq_ref.shape[1]
    heads = columns // HEAD_DIM
    observed = observed_ref.shape[0]
    capacity = key_got.shape[1]
    slots = bands * capacity
    group = grad_got.shape[1]
    blocks = mask_ref.shape[1]
    tiles = nodes // TILE
    per_tile = TILE // BLOCK
    passes = heads // HEADS_PER_PASS
    span = HEADS_PER_PASS * HEAD_DIM
    factor = 1.0 / math.sqrt(HEAD_DIM)
    low = jnp.bfloat16

    def band_peer(off):
        return lax.rem(me + off, bands)

    def band_source(off):
        return lax.rem(me + bands - off, bands)

    def model_peer(off):
        return lax.rem(mine + off, models)

    barrier = pltpu.get_barrier_semaphore()
    for off in range(1, bands):
        pl.semaphore_signal(
            barrier, inc=1, device_id={"band": band_peer(off)}, device_id_type=MESH
        )
    for off in range(1, models):
        pl.semaphore_signal(
            barrier, inc=1, device_id={"mp": model_peer(off)}, device_id_type=MESH
        )

    target = band_ref[...]
    onehot = jnp.where(
        lax.broadcasted_iota(jnp.int32, (bands, observed), 0) == target, 1.0, 0.0
    )
    before = jnp.where(
        lax.broadcasted_iota(jnp.int32, (observed, observed), 0)
        < lax.broadcasted_iota(jnp.int32, (observed, observed), 1),
        1.0,
        0.0,
    ).astype(low)
    earlier = dot_wide(onehot.astype(low), before)
    rank = jnp.sum(earlier * onehot, axis=0, keepdims=True)
    slot_row = target * capacity + rank.astype(jnp.int32)
    place = jnp.where(
        lax.broadcasted_iota(jnp.int32, (slots, observed), 0) == slot_row, 1.0, 0.0
    ).astype(low)
    keys_here = dot_wide(observed_ref[...], wk_ref[...]).astype(low)
    key_send[...] = dot_wide(place, keys_here).astype(low).reshape(bands, capacity, columns)
    cell_hot = jnp.where(
        lax.broadcasted_iota(jnp.int32, (blocks, observed), 0) == (cell_ref[...] >> 7), 1.0, 0.0
    ).astype(low)
    cell_hot = jnp.concatenate([cell_hot, jnp.zeros((16 - blocks, observed), low)], axis=0)
    hot = dot_transposed(cell_hot, place).astype(low)
    for s in range(bands):
        hot_send[s] = hot[:, s * capacity : (s + 1) * capacity]

    def incoming(kind, off, source, landing):
        return pltpu.make_async_remote_copy(
            src_ref=source,
            dst_ref=landing,
            send_sem=in_send.at[kind, off],
            recv_sem=in_recv.at[kind, off],
            device_id={"band": band_peer(off)},
            device_id_type=MESH,
        )

    def start_in(kind, source, landing):
        for off in range(1, bands):
            incoming(kind, off, source.at[band_peer(off)], landing.at[me]).start()

    def wait_in(kind, source, landing):
        for off in range(1, bands):
            incoming(kind, off, source.at[band_peer(off)], landing.at[band_source(off)]).wait()

    pl.semaphore_wait(barrier, bands + models - 2)
    start_in(0, key_send, key_got)
    start_in(1, hot_send, hot_got)
    values_here = dot_wide(observed_ref[...], wv_ref[...]).astype(low)
    value_send[...] = dot_wide(place, values_here).astype(low).reshape(bands, capacity, columns)
    start_in(2, value_send, value_got)
    grad_send[...] = (
        dot_transposed(adjoint_ref[...], wo_ref[...]).astype(low).reshape(bands, group, columns)
    )
    start_in(3, grad_send, grad_got)

    my_columns = pl.ds(pl.multiple_of(mine * columns, columns), columns)

    def adjoint_rows(q):
        return adjoint_ref.at[pl.ds(pl.multiple_of(q * group, group), group), my_columns]

    for off in range(1, bands):
        incoming(4, off, adjoint_rows(band_peer(off)), adj_got.at[me]).start()
    key_got[me] = key_send[me]
    hot_got[me] = hot_send[me]
    value_got[me] = value_send[me]
    grad_got[me] = grad_send[me]
    adj_got[me] = adjoint_ref[pl.ds(pl.multiple_of(me * group, group), group), my_columns]

    queries = (dot_wide(latents_ref[...], wq_ref[...]) * factor).astype(low)
    query_s[...] = queries
    turned = jnp.transpose(queries)
    for t in range(tiles):
        query_t[t] = turned[:, t * TILE : (t + 1) * TILE]
    skey_s[...] = dot_wide(latents_ref[...], wk_ref[...]).astype(low)
    svalue_s[...] = dot_wide(latents_ref[...], wv_ref[...]).astype(low)
    dkey_t[...] = jnp.zeros_like(dkey_t)
    dvalue_t[...] = jnp.zeros_like(dvalue_t)
    lane_head = lax.broadcasted_iota(jnp.int32, (1, columns), 1) // HEAD_DIM

    permute = jnp.where(
        lax.broadcasted_iota(jnp.int32, (nodes, nodes), 1) == column_of(map_ref[...]), 1.0, 0.0
    ).astype(low)
    slot_column = column_of(slot_row)

    def split_heads(landed, kept):
        whole = landed[...].reshape(slots, columns)
        for h in range(heads):
            kept[h] = jnp.where(lane_head == h, whole.astype(jnp.float32), 0.0).astype(low)

    wait_in(0, key_send, key_got)
    split_heads(key_got, key_heads)
    wait_in(1, hot_send, hot_got)
    hot_all = jnp.concatenate([hot_got[s] for s in range(bands)], axis=1)
    mask = jnp.concatenate(
        [mask_ref[...].astype(jnp.float32), jnp.zeros((blocks, 16 - blocks), jnp.float32)], axis=1
    ).astype(low)
    bias = jnp.where(dot_wide(mask, hot_all) > 0.5, 0.0, -1e30)
    for b in range(blocks):
        bias_s[b] = bias[b : b + 1, :]
    wait_in(2, value_send, value_got)
    split_heads(value_got, value_heads)
    wait_in(3, grad_send, grad_got)
    grads = dot_wide(permute, grad_got[...].reshape(nodes, columns)).astype(low)
    grad_s[...] = grads
    turned = jnp.transpose(grads)
    for t in range(tiles):
        grad_t[t] = turned[:, t * TILE : (t + 1) * TILE]

    def back(part, which, off, source_band, landing_band):
        rows = pl.ds(which * columns + part * span, span)
        return pltpu.make_async_remote_copy(
            src_ref=back_send.at[source_band, rows],
            dst_ref=back_got.at[landing_band, rows],
            send_sem=back_send_sem.at[part * 2 + which, off],
            recv_sem=back_recv_sem.at[part * 2 + which, off],
            device_id={"band": band_peer(off)},
            device_id_type=MESH,
        )

    def node_copy(off, t):
        return pltpu.make_async_remote_copy(
            src_ref=node_send.at[model_peer(off), t],
            dst_ref=node_got.at[off - 1, t],
            send_sem=node_send_sem.at[off - 1, t],
            recv_sem=node_recv_sem.at[off - 1, t],
            device_id={"mp": model_peer(off)},
            device_id_type=MESH,
        )

    for part in range(passes):

        def tile_step(t, carry, part=part):
            rows = pl.ds(pl.multiple_of(t * TILE, TILE), TILE)
            query = query_s[rows, :]
            grad = grad_s[rows, :]
            query_wide = query.astype(jnp.float32)
            grad_wide = grad.astype(jnp.float32)
            skey_wide = skey_s[rows, :].astype(jnp.float32)
            svalue_wide = svalue_s[rows, :].astype(jnp.float32)
            own_products = query_wide * skey_wide
            own_dproducts = grad_wide * svalue_wide
            penalty = bias_s[pl.ds(t * per_tile, per_tile)]
            if part == 0:
                dquery = jnp.zeros((TILE, columns), jnp.float32)
                own_dscores = jnp.zeros((TILE, columns), jnp.float32)
                own_probs = jnp.zeros((TILE, columns), jnp.float32)
            else:
                dquery = dquery_s[rows, :]
                own_dscores = dscore_s[rows, :]
                own_probs = prob_s[rows, :]
            for h in range(part * HEADS_PER_PASS, (part + 1) * HEADS_PER_PASS):
                lanes = lane_head == h
                keys = key_heads[h]
                scores = dot_transposed(query, keys)
                scores = (scores.reshape(per_tile, BLOCK, slots) + penalty).reshape(TILE, slots)
                own_score = jnp.sum(jnp.where(lanes, own_products, 0.0), axis=1, keepdims=True)
                own_dprob = jnp.sum(jnp.where(lanes, own_dproducts, 0.0), axis=1, keepdims=True)
                highest = jnp.maximum(jnp.max(scores, axis=1, keepdims=True), own_score)
                weights = jnp.exp(scores - highest)
                own_weight = jnp.exp(own_score - highest)
                inverse = 1.0 / (jnp.sum(weights, axis=1, keepdims=True) + own_weight)
                probs = weights * inverse
                own_prob = own_weight * inverse
                dprobs = dot_transposed(grad, value_heads[h])
                centre = jnp.sum(probs * dprobs, axis=1, keepdims=True) + own_prob * own_dprob
                dscore_low = (probs * (dprobs - centre)).astype(low)
                probs_low = probs.astype(low)
                own_dscore = own_prob * (own_dprob - centre)
                dquery = dquery + dot_wide(dscore_low, keys)
                own_dscores = jnp.where(lanes, own_dscore, own_dscores)
                own_probs = jnp.where(lanes, own_prob, own_probs)
                features = pl.ds(h * HEAD_DIM, HEAD_DIM)
                dkey_t[features, :] += dot_wide(query_t[t, features, :], dscore_low)
                dvalue_t[features, :] += dot_wide(grad_t[t, features, :], probs_low)
            if part < passes - 1:
                dquery_s[rows, :] = dquery
                dscore_s[rows, :] = own_dscores
                prob_s[rows, :] = own_probs
            else:
                pieces = jnp.concatenate(
                    [
                        ((dquery + own_dscores * skey_wide) * factor).astype(low),
                        (own_dscores * query_wide).astype(low),
                        (own_probs * grad_wide).astype(low),
                    ],
                    axis=1,
                )
                weights_all = jnp.concatenate([wq_ref[...], wk_ref[...], wv_ref[...]], axis=1)
                term = dot_transposed(pieces, weights_all).astype(low)
                for j in range(models):
                    node_send[j, t] = term[:, j * columns : (j + 1) * columns]
                for off in range(1, models):
                    node_copy(off, t).start()
            return carry

        lax.fori_loop(0, tiles, tile_step, 0)
        for which, total in ((0, dkey_t), (1, dvalue_t)):
            done = total[pl.ds(part * span, span), :].astype(low)
            for s in range(bands):
                back_send[s, pl.ds(which * columns + part * span, span), :] = done[
                    :, s * capacity : (s + 1) * capacity
                ]
            for off in range(1, bands):
                back(part, which, off, band_peer(off), me).start()
    back_got[me] = back_send[me]

    for off in range(1, bands):
        incoming(4, off, adjoint_rows(band_peer(off)), adj_got.at[band_source(off)]).wait()
    adjoint_mine = dot_wide(permute, adj_got[...].reshape(nodes, columns))
    gather = jnp.where(
        lax.broadcasted_iota(jnp.int32, (observed, slots), 1) == slot_column, 1.0, 0.0
    ).astype(low)
    for part in range(passes):
        for which in range(2):
            for off in range(1, bands):
                back(part, which, off, band_peer(off), band_source(off)).wait()
    returned = jnp.concatenate([back_got[s] for s in range(bands)], axis=1)
    own_pairs = dot_transposed(gather, returned).astype(low)
    w_pair = jnp.concatenate([wk_ref[...], wv_ref[...]], axis=1)
    obs_term = dot_transposed(own_pairs, w_pair).astype(low)
    for j in range(models):
        obs_send[j] = obs_term[:, j * columns : (j + 1) * columns]

    def obs_copy(off):
        return pltpu.make_async_remote_copy(
            src_ref=obs_send.at[model_peer(off)],
            dst_ref=obs_got.at[off - 1],
            send_sem=obs_send_sem.at[off - 1],
            recv_sem=obs_recv_sem.at[off - 1],
            device_id={"mp": model_peer(off)},
            device_id_type=MESH,
        )

    for off in range(1, models):
        obs_copy(off).start()
    for t in range(tiles):
        for off in range(1, models):
            node_copy(off, t).wait()
        rows = slice(t * TILE, (t + 1) * TILE)
        total = node_send[mine, t].astype(jnp.float32)
        for off in range(1, models):
            total = total + node_got[off - 1, t].astype(jnp.float32)
        node_out[rows, :] = (adjoint_mine[rows, :] + total).astype(low)
    total = obs_send[mine].astype(jnp.float32)
    for off in range(1, models):
        obs_copy(off).wait()
        total = total + obs_got[off - 1].astype(jnp.float32)
    observed_out[...] = total.astype(low)


def on_device(
    node_adjoint,
    band_map,
    latents,
    observations,
    route_band,
    route_cell,
    block_mask,
    w_query,
    w_key,
    w_value,
    w_out,
):
    bands = lax.axis_size("band")
    models = lax.axis_size("mp")
    nodes = latents.shape[0]
    columns = w_query.shape[1]
    heads = columns // HEAD_DIM
    observed = observations.shape[0]
    capacity = 2 * observed // bands
    slots = capacity * bands
    group = nodes // bands
    blocks = block_mask.shape[1]
    tiles = nodes // TILE
    passes = heads // HEADS_PER_PASS
    low, wide = jnp.bfloat16, jnp.float32
    dma = pltpu.SemaphoreType.DMA
    vmem = pl.BlockSpec(memory_space=pltpu.VMEM)
    return pl.pallas_call(
        functools.partial(encoder_kernel, bands, models),
        out_shape=(
            jax.ShapeDtypeStruct((nodes, columns), low),
            jax.ShapeDtypeStruct((observed, columns), low),
        ),
        in_specs=[vmem] * 11,
        out_specs=(vmem, vmem),
        scratch_shapes=[
            pltpu.VMEM((bands, capacity, columns), low),
            pltpu.VMEM((bands, capacity, columns), low),
            pltpu.VMEM((bands, 16, capacity), low),
            pltpu.VMEM((bands, group, columns), low),
            pltpu.VMEM((bands, capacity, columns), low),
            pltpu.VMEM((bands, capacity, columns), low),
            pltpu.VMEM((bands, 16, capacity), low),
            pltpu.VMEM((bands, group, columns), low),
            pltpu.VMEM((bands, group, columns), low),
            pltpu.VMEM((nodes, columns), low),
            pltpu.VMEM((tiles, columns, TILE), low),
            pltpu.VMEM((nodes, columns), low),
            pltpu.VMEM((nodes, columns), low),
            pltpu.VMEM((nodes, columns), low),
            pltpu.VMEM((tiles, columns, TILE), low),
            pltpu.VMEM((heads, slots, columns), low),
            pltpu.VMEM((heads, slots, columns), low),
            pltpu.VMEM((blocks, 1, slots), wide),
            pltpu.VMEM((columns, slots), wide),
            pltpu.VMEM((columns, slots), wide),
            pltpu.VMEM((nodes, columns), wide),
            pltpu.VMEM((nodes, columns), wide),
            pltpu.VMEM((nodes, columns), wide),
            pltpu.VMEM((bands, 2 * columns, capacity), low),
            pltpu.VMEM((bands, 2 * columns, capacity), low),
            pltpu.VMEM((models, tiles, TILE, columns), low),
            pltpu.VMEM((models - 1, tiles, TILE, columns), low),
            pltpu.VMEM((models, observed, columns), low),
            pltpu.VMEM((models - 1, observed, columns), low),
            dma((5, bands)),
            dma((5, bands)),
            dma((2 * passes, bands)),
            dma((2 * passes, bands)),
            dma((models - 1, tiles)),
            dma((models - 1, tiles)),
            dma((models - 1,)),
            dma((models - 1,)),
        ],
        compiler_params=pltpu.CompilerParams(collective_id=0, has_side_effects=True),
    )(
        node_adjoint,
        band_map,
        latents,
        observations,
        route_band.reshape(1, observed),
        route_cell.reshape(1, observed),
        block_mask,
        w_query,
        w_key,
        w_value,
        w_out,
    )


def solution(mesh):
    bands = mesh.shape["band"]

    def body(*arrays):
        capacity = 2 * arrays[3].shape[0] // bands
        group = arrays[0].shape[0] // bands
        tiled = capacity % 128 == 0 and group % 16 == 0
        return (on_device if tiled else on_device_plain)(*arrays)

    return jax.shard_map(
        body,
        mesh=mesh,
        in_specs=(
            P("band", None),
            P("band", None),
            P("band", None),
            P("band", None),
            P("band", None),
            P("band"),
            P("band", None),
            P(None, "mp"),
            P(None, "mp"),
            P(None, "mp"),
            P("mp", None),
        ),
        out_specs=(P("band", "mp"), P("band", "mp")),
        check_vma=False,
    )
```

```python
import functools
import math

import jax
import jax.numpy as jnp
from jax import lax
from jax.experimental import pallas as pl
from jax.experimental.pallas import tpu as pltpu
from jax.sharding import PartitionSpec as P

HEAD_DIM = 32
BLOCK = 128


def dot_wide(left, right):
    return jnp.dot(left, right, preferred_element_type=jnp.float32)


def dot_transposed(left, right):
    return lax.dot_general(
        left, right, (((1,), (1,)), ((), ())), preferred_element_type=jnp.float32
    )


def broaden_precision(value):
    return lax.optimization_barrier(value).astype(jnp.float32)


def send_slots(route_band, band_count, capacity):
    target = route_band[:, 0]
    onehot = (target[:, None] == jnp.arange(band_count, dtype=jnp.int32)[None, :]).astype(jnp.int32)
    earlier = jnp.cumsum(onehot, axis=0) - onehot
    rank_within = jnp.sum(earlier * onehot, axis=1)
    return target * capacity + rank_within


def on_device_plain(
    node_adjoint,
    band_map,
    latents,
    observations,
    route_band,
    route_cell,
    block_mask,
    w_query,
    w_key,
    w_value,
    w_out,
):
    band_count = lax.axis_size("band")
    node_count = latents.shape[0]
    column_count = w_query.shape[1]
    head_count = column_count // HEAD_DIM
    observed_rows = observations.shape[0]
    capacity = 2 * observed_rows // band_count
    slot_count = capacity * band_count
    block_count = block_mask.shape[1]
    model_index = lax.axis_index("mp")
    score_factor_scale = 1.0 / math.sqrt(HEAD_DIM)
    w_pair = jnp.concatenate([w_key, w_value], axis=1)
    arrival = band_map[0]
    received = lax.all_to_all(node_adjoint, "band", split_axis=0, concat_axis=0, tiled=True)
    adjoint = jnp.take(received, arrival, axis=0)
    adjoint_part = lax.dynamic_slice_in_dim(adjoint, model_index * column_count, column_count, 1)
    target_slot = send_slots(route_band, band_count, capacity)
    cell_send = jnp.full((slot_count,), -1, jnp.int32).at[target_slot].set(route_cell)
    own_rows = lax.dynamic_slice_in_dim(observations, model_index * column_count, column_count, 1)
    row_send = jnp.zeros((slot_count, column_count), jnp.bfloat16).at[target_slot].set(own_rows)
    row_arrived, slot_cells = (
        lax.all_to_all(row_send, "band", split_axis=0, concat_axis=0, tiled=True),
        lax.all_to_all(cell_send, "band", split_axis=0, concat_axis=0, tiled=True),
    )
    full_rows = lax.all_gather(row_arrived, "mp", axis=1, tiled=True)
    key_pairs = dot_wide(full_rows, w_pair).astype(jnp.bfloat16)
    key_head_split = key_pairs[:, :column_count].reshape(slot_count, head_count, HEAD_DIM)
    value_heads = key_pairs[:, column_count:].reshape(slot_count, head_count, HEAD_DIM)
    key_hot = (
        (slot_cells // BLOCK)[:, None] == jnp.arange(block_count, dtype=jnp.int32)[None, :]
    ).astype(jnp.bfloat16)
    node_mask = jnp.repeat(block_mask, BLOCK, axis=0).astype(jnp.bfloat16)
    queries = (dot_wide(latents, w_query) * score_factor_scale).astype(jnp.bfloat16)
    self_pair = dot_wide(latents, w_pair).astype(jnp.bfloat16)
    self_pair_key = self_pair[:, :column_count]
    self_value = self_pair[:, column_count:]
    grad_out = dot_transposed(adjoint, w_out).astype(jnp.bfloat16)
    block_rows = min(512, node_count)
    block_total = node_count // block_rows

    def split_blocks(value):
        return value.reshape(block_total, block_rows, head_count, HEAD_DIM)

    stacked = (
        split_blocks(queries),
        split_blocks(self_pair_key),
        split_blocks(self_value),
        split_blocks(grad_out),
        node_mask.reshape(block_total, block_rows, block_count),
    )

    def attend(running, block_entries):
        key_grad, value_grad = running
        query_tile, self_key_tile, self_value_tile, gradient_block, block_mask_tile = block_entries
        scores = jnp.einsum(
            "qhd,khd->hqk", query_tile, key_head_split, preferred_element_type=jnp.float32
        )
        allowed = (dot_transposed(block_mask_tile, key_hot) > 0.5)[None]
        query_widened = broaden_precision(query_tile)
        grad_wide = broaden_precision(gradient_block)
        self_key_widened = broaden_precision(self_key_tile)
        self_score = jnp.transpose(jnp.sum(query_widened * self_key_widened, axis=2))
        highest = jnp.maximum(jnp.max(jnp.where(allowed, scores, -jnp.inf), axis=2), self_score)
        weights = jnp.where(allowed, jnp.exp(scores - highest[:, :, None]), 0.0)
        own_weight = jnp.exp(self_score - highest)
        normaliser = jnp.sum(weights, axis=2) + own_weight
        probabilities = weights / normaliser[:, :, None]
        own_prob = own_weight / normaliser
        probabilities_low = probabilities.astype(jnp.bfloat16)
        dprobs = jnp.einsum(
            "qhd,khd->hqk", gradient_block, value_heads, preferred_element_type=jnp.float32
        )
        own_dprob = jnp.transpose(jnp.sum(grad_wide * broaden_precision(self_value_tile), axis=2))
        centre = jnp.sum(probabilities * dprobs, axis=2) + own_prob * own_dprob
        dscore = probabilities * (dprobs - centre[:, :, None])
        own_dscore = own_prob * (own_dprob - centre)
        score_gradient_narrow = dscore.astype(jnp.bfloat16)
        self_score_gradient_rows = jnp.transpose(own_dscore)[:, :, None]
        own_prob_rows = jnp.transpose(own_prob)[:, :, None]
        query_gradient = jnp.einsum(
            "hqk,khd->qhd",
            score_gradient_narrow,
            key_head_split,
            preferred_element_type=jnp.float32,
        )
        query_gradient = (
            (query_gradient + self_score_gradient_rows * self_key_widened) * score_factor_scale
        ).astype(jnp.bfloat16)
        dself_key = (self_score_gradient_rows * query_widened).astype(jnp.bfloat16)
        dself_value = (own_prob_rows * grad_wide).astype(jnp.bfloat16)
        key_grad = key_grad + jnp.einsum(
            "hqk,qhd->khd", score_gradient_narrow, query_tile, preferred_element_type=jnp.float32
        )
        value_grad = value_grad + jnp.einsum(
            "hqk,qhd->khd", probabilities_low, gradient_block, preferred_element_type=jnp.float32
        )
        flat_shape = (block_rows, column_count)
        node_pieces = jnp.concatenate(
            [
                query_gradient.reshape(flat_shape),
                dself_key.reshape(flat_shape),
                dself_value.reshape(flat_shape),
            ],
            axis=1,
        )
        return ((key_grad, value_grad), node_pieces)

    zero_grads = jnp.zeros((slot_count, head_count, HEAD_DIM), jnp.float32)
    (key_grad, value_grad), node_pieces = lax.scan(attend, (zero_grads, zero_grads), stacked)
    node_pieces = node_pieces.reshape(node_count, 3 * column_count)
    w_triple = jnp.concatenate([w_query, w_key, w_value], axis=1)
    node_term = dot_transposed(node_pieces, w_triple)
    node_sum = lax.psum_scatter(
        node_term.astype(jnp.bfloat16), "mp", scatter_dimension=1, tiled=True
    ).astype(jnp.float32)
    node_grad = (adjoint_part.astype(jnp.float32) + node_sum).astype(jnp.bfloat16)
    grad_pairs = jnp.concatenate(
        [
            key_grad.astype(jnp.bfloat16).reshape(slot_count, column_count),
            value_grad.astype(jnp.bfloat16).reshape(slot_count, column_count),
        ],
        axis=1,
    )
    slot_term = dot_transposed(grad_pairs, w_pair)
    slot_sum = lax.psum_scatter(
        slot_term.astype(jnp.bfloat16), "mp", scatter_dimension=1, tiled=True
    )
    returned = lax.all_to_all(slot_sum, "band", split_axis=0, concat_axis=0, tiled=True)
    observation_grad = jnp.take(returned, target_slot, axis=0)
    return (node_grad, observation_grad)


TILE = 256
HEADS_PER_PASS = 1
UNROLL = 2
MESH = pl.DeviceIdType.MESH


def dot_first(left, right):
    return lax.dot_general(
        left, right, (((0,), (0,)), ((), ())), preferred_element_type=jnp.float32
    )


def column_of(row, rows=128):
    wide = jnp.transpose(jnp.broadcast_to(row.astype(jnp.float32), (rows, row.shape[1])))
    return wide[:, :1].astype(jnp.int32)


def encoder_kernel(
    bands,
    models,
    adjoint_ref,
    map_ref,
    latents_ref,
    observed_ref,
    band_ref,
    cell_ref,
    mask_ref,
    wq_ref,
    wk_ref,
    wv_ref,
    wo_ref,
    node_out,
    observed_out,
    row_send,
    hot_send,
    grad_send,
    row_got,
    hot_got,
    grad_got,
    adj_got,
    query_s,
    query_t,
    skey_s,
    svalue_s,
    grad_s,
    grad_t,
    key_heads,
    value_heads,
    bias_s,
    dkey_t,
    dvalue_t,
    dquery_s,
    dscore_s,
    prob_s,
    back_send,
    back_got,
    node_send,
    node_pair,
    node_sum,
    node_got,
    obs_send,
    obs_pair,
    obs_sum,
    obs_got,
    in_send,
    in_recv,
    row_send_sem,
    row_recv_sem,
    back_send_sem,
    back_recv_sem,
    node_send_sem,
    node_recv_sem,
    pair_send_sem,
    pair_recv_sem,
):
    me = lax.axis_index("band")
    mine = lax.axis_index("mp")
    nodes = latents_ref.shape[0]
    columns = wq_ref.shape[1]
    heads = columns // HEAD_DIM
    observed = observed_ref.shape[0]
    capacity = row_got.shape[2]
    slots = bands * capacity
    group = grad_got.shape[1]
    blocks = mask_ref.shape[1]
    tiles = nodes // TILE
    per_tile = TILE // BLOCK
    passes = heads // HEADS_PER_PASS
    span = HEADS_PER_PASS * HEAD_DIM
    factor = 1.0 / math.sqrt(HEAD_DIM)
    low = jnp.bfloat16

    def band_peer(off):
        return lax.rem(me + off, bands)

    def band_source(off):
        return lax.rem(me + bands - off, bands)

    def model_peer(off):
        return lax.rem(mine + off, models)

    def model_source(off):
        return lax.rem(mine + models - off, models)

    chips = models // 2
    side = lax.rem(mine, 2)
    chip = mine // 2
    partner = mine + 1 - 2 * side
    my_columns = pl.ds(pl.multiple_of(mine * columns, columns), columns)

    def chip_peer(off):
        return lax.rem(chip + off, chips)

    barrier = pltpu.get_barrier_semaphore()
    for off in range(1, bands):
        pl.semaphore_signal(
            barrier, inc=1, device_id={"band": band_peer(off)}, device_id_type=MESH
        )
    for off in range(1, models):
        pl.semaphore_signal(
            barrier, inc=1, device_id={"mp": model_peer(off)}, device_id_type=MESH
        )

    target = band_ref[...]
    onehot = jnp.where(
        lax.broadcasted_iota(jnp.int32, (bands, observed), 0) == target, 1.0, 0.0
    )
    before = jnp.where(
        lax.broadcasted_iota(jnp.int32, (observed, observed), 0)
        < lax.broadcasted_iota(jnp.int32, (observed, observed), 1),
        1.0,
        0.0,
    ).astype(low)
    earlier = dot_wide(onehot.astype(low), before)
    rank = jnp.sum(earlier * onehot, axis=0, keepdims=True)
    slot_row = target * capacity + rank.astype(jnp.int32)
    place = jnp.where(
        lax.broadcasted_iota(jnp.int32, (slots, observed), 0) == slot_row, 1.0, 0.0
    ).astype(low)
    row_send[...] = (
        dot_wide(place, observed_ref[:, my_columns]).astype(low).reshape(bands, capacity, columns)
    )
    cell_hot = jnp.where(
        lax.broadcasted_iota(jnp.int32, (blocks, observed), 0) == (cell_ref[...] >> 7), 1.0, 0.0
    ).astype(low)
    cell_hot = jnp.concatenate([cell_hot, jnp.zeros((16 - blocks, observed), low)], axis=0)
    hot = dot_transposed(cell_hot, place).astype(low)
    for s in range(bands):
        hot_send[s] = hot[:, s * capacity : (s + 1) * capacity]

    def incoming(kind, off, source, landing):
        return pltpu.make_async_remote_copy(
            src_ref=source,
            dst_ref=landing,
            send_sem=in_send.at[kind, off],
            recv_sem=in_recv.at[kind, off],
            device_id={"band": band_peer(off)},
            device_id_type=MESH,
        )

    def start_in(kind, source, landing):
        for off in range(1, bands):
            incoming(kind, off, source.at[band_peer(off)], landing.at[me]).start()

    def wait_in(kind, source, landing):
        for off in range(1, bands):
            incoming(kind, off, source.at[band_peer(off)], landing.at[band_source(off)]).wait()

    def arrived(off):
        return incoming(0, off, row_send.at[band_peer(off)], row_got.at[mine, band_source(off)])

    def forward(off, hop, owner):
        block = row_got.at[owner, band_source(off)]
        return pltpu.make_async_remote_copy(
            src_ref=block,
            dst_ref=block,
            send_sem=row_send_sem.at[hop - 1, off],
            recv_sem=row_recv_sem.at[hop - 1, off],
            device_id={"mp": model_peer(hop)},
            device_id_type=MESH,
        )

    def adjoint_rows(q):
        return adjoint_ref.at[pl.ds(pl.multiple_of(q * group, group), group), my_columns]

    row_got[mine, me] = row_send[me]
    pl.semaphore_wait(barrier, bands + models - 2)
    start_in(0, row_send, row_got.at[mine])
    start_in(1, hot_send, hot_got)
    for hop in range(1, models):
        forward(0, hop, mine).start()
    grad_send[...] = (
        dot_transposed(adjoint_ref[...], wo_ref[...]).astype(low).reshape(bands, group, columns)
    )
    start_in(2, grad_send, grad_got)
    for off in range(1, bands):
        incoming(3, off, adjoint_rows(band_peer(off)), adj_got.at[me]).start()

    def pass_on(off):
        arrived(off).wait_recv()
        for hop in range(1, models):
            forward(off, hop, mine).start()

    hot_got[me] = hot_send[me]
    grad_got[me] = grad_send[me]
    adj_got[me] = adjoint_ref[pl.ds(pl.multiple_of(me * group, group), group), my_columns]
    queries = (dot_wide(latents_ref[...], wq_ref[...]) * factor).astype(low)
    query_s[...] = queries
    turned = jnp.transpose(queries)
    for t in range(tiles):
        query_t[t] = turned[:, t * TILE : (t + 1) * TILE]
    for off in range(1, bands // 2):
        pass_on(off)
    skey_s[...] = dot_wide(latents_ref[...], wk_ref[...]).astype(low)
    svalue_s[...] = dot_wide(latents_ref[...], wv_ref[...]).astype(low)
    dkey_t[...] = jnp.zeros_like(dkey_t)
    dvalue_t[...] = jnp.zeros_like(dvalue_t)
    for off in range(bands // 2, bands):
        pass_on(off)
    lane_head = lax.broadcasted_iota(jnp.int32, (1, columns), 1) // HEAD_DIM

    permute = jnp.where(
        lax.broadcasted_iota(jnp.int32, (nodes, nodes), 1) == column_of(map_ref[...]), 1.0, 0.0
    ).astype(low)
    slot_column = column_of(slot_row)

    def split_heads(weights, kept):
        whole = jnp.zeros((slots, columns), jnp.float32)
        for j in range(models):
            whole = whole + dot_wide(
                row_got[j].reshape(slots, columns), weights[j * columns : (j + 1) * columns, :]
            )
        whole = whole.astype(low).astype(jnp.float32)
        for h in range(heads):
            kept[h] = jnp.where(lane_head == h, whole, 0.0).astype(low)

    wait_in(1, hot_send, hot_got)
    hot_all = jnp.concatenate([hot_got[s] for s in range(bands)], axis=1)
    mask = jnp.concatenate(
        [mask_ref[...].astype(jnp.float32), jnp.zeros((blocks, 16 - blocks), jnp.float32)], axis=1
    ).astype(low)
    bias = jnp.where(dot_wide(mask, hot_all) > 0.5, 0.0, -1e30)
    for b in range(blocks):
        bias_s[b] = bias[b : b + 1, :]
    for off in range(bands):
        for hop in range(1, models):
            forward(off, hop, model_source(hop)).wait_recv()
    split_heads(wk_ref, key_heads)
    split_heads(wv_ref, value_heads)
    wait_in(2, grad_send, grad_got)
    grads = dot_wide(permute, grad_got[...].reshape(nodes, columns)).astype(low)
    grad_s[...] = grads
    turned = jnp.transpose(grads)
    for t in range(tiles):
        grad_t[t] = turned[:, t * TILE : (t + 1) * TILE]

    def back(part, which, off, source_band, landing_band):
        rows = pl.ds(which * columns + part * span, span)
        return pltpu.make_async_remote_copy(
            src_ref=back_send.at[source_band, rows],
            dst_ref=back_got.at[landing_band, rows],
            send_sem=back_send_sem.at[part * 2 + which, off],
            recv_sem=back_recv_sem.at[part * 2 + which, off],
            device_id={"band": band_peer(off)},
            device_id_type=MESH,
        )

    def pair_copy(source, landing, index):
        return pltpu.make_async_remote_copy(
            src_ref=source,
            dst_ref=landing,
            send_sem=pair_send_sem.at[index],
            recv_sem=pair_recv_sem.at[index],
            device_id={"mp": partner},
            device_id_type=MESH,
        )

    def cross_copy(off, source, landing, index):
        return pltpu.make_async_remote_copy(
            src_ref=source,
            dst_ref=landing,
            send_sem=node_send_sem.at[off - 1, index],
            recv_sem=node_recv_sem.at[off - 1, index],
            device_id={"mp": chip_peer(off) * 2 + side},
            device_id_type=MESH,
        )

    def node_exchange(t):
        return pair_copy(node_send.at[1 - side, t], node_pair.at[t], t)

    def node_cross(off, t):
        return cross_copy(off, node_sum.at[off - 1, t], node_got.at[off - 1, t], t)

    def obs_exchange():
        return pair_copy(obs_send.at[1 - side], obs_pair, tiles)

    def obs_cross(off):
        return cross_copy(off, obs_sum.at[off - 1], obs_got.at[off - 1], tiles)

    def node_reduce(t):
        node_exchange(t).wait()
        for off in range(1, chips):
            c = chip_peer(off)
            node_sum[off - 1, t] = (
                node_send[side, t, c].astype(jnp.float32) + node_pair[t, c].astype(jnp.float32)
            ).astype(low)
            node_cross(off, t).start()

    for part in range(passes):

        def tile_step(t, part=part):
            rows = pl.ds(pl.multiple_of(t * TILE, TILE), TILE)
            query = query_s[rows, :]
            grad = grad_s[rows, :]
            query_wide = query.astype(jnp.float32)
            grad_wide = grad.astype(jnp.float32)
            skey_wide = skey_s[rows, :].astype(jnp.float32)
            svalue_wide = svalue_s[rows, :].astype(jnp.float32)
            own_products = query_wide * skey_wide
            own_dproducts = grad_wide * svalue_wide
            penalty = bias_s[pl.ds(t * per_tile, per_tile)]
            if part == 0:
                dquery = jnp.zeros((TILE, columns), jnp.float32)
                own_dscores = jnp.zeros((TILE, columns), jnp.float32)
                own_probs = jnp.zeros((TILE, columns), jnp.float32)
            else:
                dquery = dquery_s[rows, :]
                own_dscores = dscore_s[rows, :]
                own_probs = prob_s[rows, :]
            for h in range(part * HEADS_PER_PASS, (part + 1) * HEADS_PER_PASS):
                lanes = lane_head == h
                keys = key_heads[h]
                scores = dot_transposed(query, keys)
                scores = (scores.reshape(per_tile, BLOCK, slots) + penalty).reshape(TILE, slots)
                own_score = jnp.sum(jnp.where(lanes, own_products, 0.0), axis=1, keepdims=True)
                own_dprob = jnp.sum(jnp.where(lanes, own_dproducts, 0.0), axis=1, keepdims=True)
                highest = jnp.maximum(jnp.max(scores, axis=1, keepdims=True), own_score)
                weights = jnp.exp(scores - highest)
                own_weight = jnp.exp(own_score - highest)
                inverse = 1.0 / (jnp.sum(weights, axis=1, keepdims=True) + own_weight)
                probs = weights * inverse
                own_prob = own_weight * inverse
                dprobs = dot_transposed(grad, value_heads[h])
                centre = jnp.sum(probs * dprobs, axis=1, keepdims=True) + own_prob * own_dprob
                dscore_low = (probs * (dprobs - centre)).astype(low)
                probs_low = probs.astype(low)
                own_dscore = own_prob * (own_dprob - centre)
                dquery = dquery + dot_wide(dscore_low, keys)
                own_dscores = jnp.where(lanes, own_dscore, own_dscores)
                own_probs = jnp.where(lanes, own_prob, own_probs)
                features = pl.ds(h * HEAD_DIM, HEAD_DIM)
                dkey_t[features, :] += dot_wide(query_t[t, features, :], dscore_low)
                dvalue_t[features, :] += dot_wide(grad_t[t, features, :], probs_low)
            if part < passes - 1:
                dquery_s[rows, :] = dquery
                dscore_s[rows, :] = own_dscores
                prob_s[rows, :] = own_probs
            else:
                pieces = jnp.concatenate(
                    [
                        ((dquery + own_dscores * skey_wide) * factor).astype(low),
                        (own_dscores * query_wide).astype(low),
                        (own_probs * grad_wide).astype(low),
                    ],
                    axis=1,
                )
                weights_all = jnp.concatenate([wq_ref[...], wk_ref[...], wv_ref[...]], axis=1)
                term = dot_transposed(pieces, weights_all).astype(low)
                for j in range(models):
                    node_send[j % 2, t, j // 2] = term[:, j * columns : (j + 1) * columns]
                node_exchange(t).start()

        if part < passes - 1:

            def some_tiles(i, carry):
                for u in range(UNROLL):
                    tile_step(i * UNROLL + u)
                return carry

            lax.fori_loop(0, tiles // UNROLL, some_tiles, 0)
        else:
            for t in range(tiles):
                tile_step(t)
                if t >= UNROLL:
                    node_reduce(t - UNROLL)
        for which, total in ((0, dkey_t), (1, dvalue_t)):
            done = total[pl.ds(part * span, span), :].astype(low)
            for s in range(bands):
                back_send[s, pl.ds(which * columns + part * span, span), :] = done[
                    :, s * capacity : (s + 1) * capacity
                ]
            for off in range(1, bands):
                back(part, which, off, band_peer(off), me).start()
    back_got[me] = back_send[me]
    for t in range(tiles - UNROLL, tiles):
        node_reduce(t)

    for off in range(1, bands):
        incoming(3, off, adjoint_rows(band_peer(off)), adj_got.at[band_source(off)]).wait()
    adjoint_mine = dot_wide(permute, adj_got[...].reshape(nodes, columns))
    gather = jnp.where(
        lax.broadcasted_iota(jnp.int32, (observed, slots), 1) == slot_column, 1.0, 0.0
    ).astype(low)
    for part in range(passes):
        for which in range(2):
            for off in range(1, bands):
                back(part, which, off, band_peer(off), band_source(off)).wait()
    returned = jnp.concatenate([back_got[s] for s in range(bands)], axis=1)
    own_pairs = dot_transposed(gather, returned).astype(low)
    w_pair = jnp.concatenate([wk_ref[...], wv_ref[...]], axis=1)
    obs_term = dot_transposed(own_pairs, w_pair).astype(low)
    for j in range(models):
        obs_send[j % 2, j // 2] = obs_term[:, j * columns : (j + 1) * columns]
    obs_exchange().start()
    obs_exchange().wait()
    for off in range(1, chips):
        c = chip_peer(off)
        obs_sum[off - 1] = (
            obs_send[side, c].astype(jnp.float32) + obs_pair[c].astype(jnp.float32)
        ).astype(low)
        obs_cross(off).start()
    for t in range(tiles):
        rows = slice(t * TILE, (t + 1) * TILE)
        total = node_send[side, t, chip].astype(jnp.float32)
        total = total + node_pair[t, chip].astype(jnp.float32)
        for off in range(1, chips):
            node_cross(off, t).wait()
            total = total + node_got[off - 1, t].astype(jnp.float32)
        node_out[rows, :] = (adjoint_mine[rows, :] + total).astype(low)
    for off in range(1, bands):
        arrived(off).wait_send()
    for off in range(bands):
        for hop in range(1, models):
            forward(off, hop, mine).wait_send()
    total = obs_send[side, chip].astype(jnp.float32) + obs_pair[chip].astype(jnp.float32)
    for off in range(1, chips):
        obs_cross(off).wait()
        total = total + obs_got[off - 1].astype(jnp.float32)
    observed_out[...] = total.astype(low)


def on_device(
    node_adjoint,
    band_map,
    latents,
    observations,
    route_band,
    route_cell,
    block_mask,
    w_query,
    w_key,
    w_value,
    w_out,
):
    bands = lax.axis_size("band")
    models = lax.axis_size("mp")
    chips = models // 2
    nodes = latents.shape[0]
    columns = w_query.shape[1]
    heads = columns // HEAD_DIM
    observed = observations.shape[0]
    capacity = 2 * observed // bands
    slots = capacity * bands
    group = nodes // bands
    blocks = block_mask.shape[1]
    tiles = nodes // TILE
    passes = heads // HEADS_PER_PASS
    low, wide = jnp.bfloat16, jnp.float32
    dma = pltpu.SemaphoreType.DMA
    vmem = pl.BlockSpec(memory_space=pltpu.VMEM)
    return pl.pallas_call(
        functools.partial(encoder_kernel, bands, models),
        out_shape=(
            jax.ShapeDtypeStruct((nodes, columns), low),
            jax.ShapeDtypeStruct((observed, columns), low),
        ),
        in_specs=[vmem] * 11,
        out_specs=(vmem, vmem),
        scratch_shapes=[
            pltpu.VMEM((bands, capacity, columns), low),
            pltpu.VMEM((bands, 16, capacity), low),
            pltpu.VMEM((bands, group, columns), low),
            pltpu.VMEM((models, bands, capacity, columns), low),
            pltpu.VMEM((bands, 16, capacity), low),
            pltpu.VMEM((bands, group, columns), low),
            pltpu.VMEM((bands, group, columns), low),
            pltpu.VMEM((nodes, columns), low),
            pltpu.VMEM((tiles, columns, TILE), low),
            pltpu.VMEM((nodes, columns), low),
            pltpu.VMEM((nodes, columns), low),
            pltpu.VMEM((nodes, columns), low),
            pltpu.VMEM((tiles, columns, TILE), low),
            pltpu.VMEM((heads, slots, columns), low),
            pltpu.VMEM((heads, slots, columns), low),
            pltpu.VMEM((blocks, 1, slots), wide),
            pltpu.VMEM((columns, slots), wide),
            pltpu.VMEM((columns, slots), wide),
            pltpu.VMEM((nodes, columns), wide),
            pltpu.VMEM((nodes, columns), wide),
            pltpu.VMEM((nodes, columns), wide),
            pltpu.VMEM((bands, 2 * columns, capacity), low),
            pltpu.VMEM((bands, 2 * columns, capacity), low),
            pltpu.VMEM((2, tiles, chips, TILE, columns), low),
            pltpu.VMEM((tiles, chips, TILE, columns), low),
            pltpu.VMEM((chips - 1, tiles, TILE, columns), low),
            pltpu.VMEM((chips - 1, tiles, TILE, columns), low),
            pltpu.VMEM((2, chips, observed, columns), low),
            pltpu.VMEM((chips, observed, columns), low),
            pltpu.VMEM((chips - 1, observed, columns), low),
            pltpu.VMEM((chips - 1, observed, columns), low),
            dma((4, bands)),
            dma((4, bands)),
            dma((models - 1, bands)),
            dma((models - 1, bands)),
            dma((2 * passes, bands)),
            dma((2 * passes, bands)),
            dma((chips - 1, tiles + 1)),
            dma((chips - 1, tiles + 1)),
            dma((tiles + 1,)),
            dma((tiles + 1,)),
        ],
        compiler_params=pltpu.CompilerParams(collective_id=0, has_side_effects=True),
    )(
        node_adjoint,
        band_map,
        latents,
        observations,
        route_band.reshape(1, observed),
        route_cell.reshape(1, observed),
        block_mask,
        w_query,
        w_key,
        w_value,
        w_out,
    )


def solution(mesh):
    bands = mesh.shape["band"]

    def body(*arrays):
        capacity = 2 * arrays[3].shape[0] // bands
        group = arrays[0].shape[0] // bands
        tiled = capacity % 128 == 0 and group % 16 == 0
        return (on_device if tiled else on_device_plain)(*arrays)

    return jax.shard_map(
        body,
        mesh=mesh,
        in_specs=(
            P("band", None),
            P("band", None),
            P("band", None),
            P("band", None),
            P("band", None),
            P("band"),
            P("band", None),
            P(None, "mp"),
            P(None, "mp"),
            P(None, "mp"),
            P("mp", None),
        ),
        out_specs=(P("band", "mp"), P("band", "mp")),
        check_vma=False,
    )
```

```python
import functools
import math

import jax
import jax.numpy as jnp
from jax import lax
from jax.experimental import pallas as pl
from jax.experimental.pallas import tpu as pltpu
from jax.sharding import PartitionSpec as P

HEAD_DIM = 32
BLOCK = 128


def dot_wide(left, right):
    return jnp.dot(left, right, preferred_element_type=jnp.float32)


def dot_transposed(left, right):
    return lax.dot_general(
        left, right, (((1,), (1,)), ((), ())), preferred_element_type=jnp.float32
    )


def broaden_precision(value):
    return lax.optimization_barrier(value).astype(jnp.float32)


def send_slots(route_band, band_count, capacity):
    target = route_band[:, 0]
    onehot = (target[:, None] == jnp.arange(band_count, dtype=jnp.int32)[None, :]).astype(jnp.int32)
    earlier = jnp.cumsum(onehot, axis=0) - onehot
    rank_within = jnp.sum(earlier * onehot, axis=1)
    return target * capacity + rank_within


def on_device_plain(
    node_adjoint,
    band_map,
    latents,
    observations,
    route_band,
    route_cell,
    block_mask,
    w_query,
    w_key,
    w_value,
    w_out,
):
    band_count = lax.axis_size("band")
    node_count = latents.shape[0]
    column_count = w_query.shape[1]
    head_count = column_count // HEAD_DIM
    observed_rows = observations.shape[0]
    capacity = 2 * observed_rows // band_count
    slot_count = capacity * band_count
    block_count = block_mask.shape[1]
    model_index = lax.axis_index("mp")
    score_factor_scale = 1.0 / math.sqrt(HEAD_DIM)
    w_pair = jnp.concatenate([w_key, w_value], axis=1)
    arrival = band_map[0]
    received = lax.all_to_all(node_adjoint, "band", split_axis=0, concat_axis=0, tiled=True)
    adjoint = jnp.take(received, arrival, axis=0)
    adjoint_part = lax.dynamic_slice_in_dim(adjoint, model_index * column_count, column_count, 1)
    target_slot = send_slots(route_band, band_count, capacity)
    cell_send = jnp.full((slot_count,), -1, jnp.int32).at[target_slot].set(route_cell)
    own_rows = lax.dynamic_slice_in_dim(observations, model_index * column_count, column_count, 1)
    row_send = jnp.zeros((slot_count, column_count), jnp.bfloat16).at[target_slot].set(own_rows)
    row_arrived, slot_cells = (
        lax.all_to_all(row_send, "band", split_axis=0, concat_axis=0, tiled=True),
        lax.all_to_all(cell_send, "band", split_axis=0, concat_axis=0, tiled=True),
    )
    full_rows = lax.all_gather(row_arrived, "mp", axis=1, tiled=True)
    key_pairs = dot_wide(full_rows, w_pair).astype(jnp.bfloat16)
    key_head_split = key_pairs[:, :column_count].reshape(slot_count, head_count, HEAD_DIM)
    value_heads = key_pairs[:, column_count:].reshape(slot_count, head_count, HEAD_DIM)
    key_hot = (
        (slot_cells // BLOCK)[:, None] == jnp.arange(block_count, dtype=jnp.int32)[None, :]
    ).astype(jnp.bfloat16)
    node_mask = jnp.repeat(block_mask, BLOCK, axis=0).astype(jnp.bfloat16)
    queries = (dot_wide(latents, w_query) * score_factor_scale).astype(jnp.bfloat16)
    self_pair = dot_wide(latents, w_pair).astype(jnp.bfloat16)
    self_pair_key = self_pair[:, :column_count]
    self_value = self_pair[:, column_count:]
    grad_out = dot_transposed(adjoint, w_out).astype(jnp.bfloat16)
    block_rows = min(512, node_count)
    block_total = node_count // block_rows

    def split_blocks(value):
        return value.reshape(block_total, block_rows, head_count, HEAD_DIM)

    stacked = (
        split_blocks(queries),
        split_blocks(self_pair_key),
        split_blocks(self_value),
        split_blocks(grad_out),
        node_mask.reshape(block_total, block_rows, block_count),
    )

    def attend(running, block_entries):
        key_grad, value_grad = running
        query_tile, self_key_tile, self_value_tile, gradient_block, block_mask_tile = block_entries
        scores = jnp.einsum(
            "qhd,khd->hqk", query_tile, key_head_split, preferred_element_type=jnp.float32
        )
        allowed = (dot_transposed(block_mask_tile, key_hot) > 0.5)[None]
        query_widened = broaden_precision(query_tile)
        grad_wide = broaden_precision(gradient_block)
        self_key_widened = broaden_precision(self_key_tile)
        self_score = jnp.transpose(jnp.sum(query_widened * self_key_widened, axis=2))
        highest = jnp.maximum(jnp.max(jnp.where(allowed, scores, -jnp.inf), axis=2), self_score)
        weights = jnp.where(allowed, jnp.exp(scores - highest[:, :, None]), 0.0)
        own_weight = jnp.exp(self_score - highest)
        normaliser = jnp.sum(weights, axis=2) + own_weight
        probabilities = weights / normaliser[:, :, None]
        own_prob = own_weight / normaliser
        probabilities_low = probabilities.astype(jnp.bfloat16)
        dprobs = jnp.einsum(
            "qhd,khd->hqk", gradient_block, value_heads, preferred_element_type=jnp.float32
        )
        own_dprob = jnp.transpose(jnp.sum(grad_wide * broaden_precision(self_value_tile), axis=2))
        centre = jnp.sum(probabilities * dprobs, axis=2) + own_prob * own_dprob
        dscore = probabilities * (dprobs - centre[:, :, None])
        own_dscore = own_prob * (own_dprob - centre)
        score_gradient_narrow = dscore.astype(jnp.bfloat16)
        self_score_gradient_rows = jnp.transpose(own_dscore)[:, :, None]
        own_prob_rows = jnp.transpose(own_prob)[:, :, None]
        query_gradient = jnp.einsum(
            "hqk,khd->qhd",
            score_gradient_narrow,
            key_head_split,
            preferred_element_type=jnp.float32,
        )
        query_gradient = (
            (query_gradient + self_score_gradient_rows * self_key_widened) * score_factor_scale
        ).astype(jnp.bfloat16)
        dself_key = (self_score_gradient_rows * query_widened).astype(jnp.bfloat16)
        dself_value = (own_prob_rows * grad_wide).astype(jnp.bfloat16)
        key_grad = key_grad + jnp.einsum(
            "hqk,qhd->khd", score_gradient_narrow, query_tile, preferred_element_type=jnp.float32
        )
        value_grad = value_grad + jnp.einsum(
            "hqk,qhd->khd", probabilities_low, gradient_block, preferred_element_type=jnp.float32
        )
        flat_shape = (block_rows, column_count)
        node_pieces = jnp.concatenate(
            [
                query_gradient.reshape(flat_shape),
                dself_key.reshape(flat_shape),
                dself_value.reshape(flat_shape),
            ],
            axis=1,
        )
        return ((key_grad, value_grad), node_pieces)

    zero_grads = jnp.zeros((slot_count, head_count, HEAD_DIM), jnp.float32)
    (key_grad, value_grad), node_pieces = lax.scan(attend, (zero_grads, zero_grads), stacked)
    node_pieces = node_pieces.reshape(node_count, 3 * column_count)
    w_triple = jnp.concatenate([w_query, w_key, w_value], axis=1)
    node_term = dot_transposed(node_pieces, w_triple)
    node_sum = lax.psum_scatter(
        node_term.astype(jnp.bfloat16), "mp", scatter_dimension=1, tiled=True
    ).astype(jnp.float32)
    node_grad = (adjoint_part.astype(jnp.float32) + node_sum).astype(jnp.bfloat16)
    grad_pairs = jnp.concatenate(
        [
            key_grad.astype(jnp.bfloat16).reshape(slot_count, column_count),
            value_grad.astype(jnp.bfloat16).reshape(slot_count, column_count),
        ],
        axis=1,
    )
    slot_term = dot_transposed(grad_pairs, w_pair)
    slot_sum = lax.psum_scatter(
        slot_term.astype(jnp.bfloat16), "mp", scatter_dimension=1, tiled=True
    )
    returned = lax.all_to_all(slot_sum, "band", split_axis=0, concat_axis=0, tiled=True)
    observation_grad = jnp.take(returned, target_slot, axis=0)
    return (node_grad, observation_grad)


TILE = 256
HEADS_PER_PASS = 1
UNROLL = 2
MESH = pl.DeviceIdType.MESH


def dot_first(left, right):
    return lax.dot_general(
        left, right, (((0,), (0,)), ((), ())), preferred_element_type=jnp.float32
    )


def column_of(row, rows=128):
    wide = jnp.transpose(jnp.broadcast_to(row.astype(jnp.float32), (rows, row.shape[1])))
    return wide[:, :1].astype(jnp.int32)


def encoder_kernel(
    bands,
    models,
    adjoint_hbm,
    map_ref,
    latents_hbm,
    observed_hbm,
    band_ref,
    cell_ref,
    mask_ref,
    wq_hbm,
    wk_hbm,
    wv_hbm,
    wo_hbm,
    node_out,
    observed_out,
    adjoint_ref,
    latents_ref,
    observed_ref,
    wq_ref,
    wk_ref,
    wv_ref,
    wo_ref,
    load_sem,
    row_send,
    hot_send,
    grad_send,
    row_got,
    hot_got,
    grad_got,
    adj_got,
    query_s,
    query_t,
    skey_s,
    svalue_s,
    grad_s,
    grad_t,
    key_heads,
    value_heads,
    bias_s,
    dkey_t,
    dvalue_t,
    dscore_low_s,
    dscore_s,
    prob_s,
    permute_s,
    gather_s,
    own_s,
    back_send,
    back_got,
    node_send,
    node_pair,
    node_sum,
    node_got,
    obs_send,
    obs_pair,
    obs_sum,
    obs_got,
    in_send,
    in_recv,
    row_send_sem,
    row_recv_sem,
    back_send_sem,
    back_recv_sem,
    node_send_sem,
    node_recv_sem,
    pair_send_sem,
    pair_recv_sem,
):
    me = lax.axis_index("band")
    mine = lax.axis_index("mp")
    nodes = latents_ref.shape[0]
    columns = wq_ref.shape[1]
    heads = columns // HEAD_DIM
    observed = observed_ref.shape[0]
    capacity = row_got.shape[2]
    slots = bands * capacity
    group = grad_got.shape[1]
    blocks = mask_ref.shape[1]
    tiles = nodes // TILE
    per_tile = TILE // BLOCK
    passes = heads // HEADS_PER_PASS
    span = HEADS_PER_PASS * HEAD_DIM
    factor = 1.0 / math.sqrt(HEAD_DIM)
    low = jnp.bfloat16

    def band_peer(off):
        return lax.rem(me + off, bands)

    def band_source(off):
        return lax.rem(me + bands - off, bands)

    def model_peer(off):
        return lax.rem(mine + off, models)

    def model_source(off):
        return lax.rem(mine + models - off, models)

    chips = models // 2
    side = lax.rem(mine, 2)
    chip = mine // 2
    partner = mine + 1 - 2 * side
    my_columns = pl.ds(pl.multiple_of(mine * columns, columns), columns)

    def chip_peer(off):
        return lax.rem(chip + off, chips)

    loads = {}
    for index, (name, source, landing) in enumerate(
        (
            ("observed", observed_hbm, observed_ref),
            ("adjoint", adjoint_hbm, adjoint_ref),
            ("wo", wo_hbm, wo_ref),
            ("latents", latents_hbm, latents_ref),
            ("wq", wq_hbm, wq_ref),
            ("wk", wk_hbm, wk_ref),
            ("wv", wv_hbm, wv_ref),
        )
    ):
        loads[name] = pltpu.make_async_copy(source, landing, load_sem.at[index])

    barrier = pltpu.get_barrier_semaphore()
    for off in range(1, bands):
        pl.semaphore_signal(
            barrier, inc=1, device_id={"band": band_peer(off)}, device_id_type=MESH
        )
    for off in range(1, models):
        pl.semaphore_signal(
            barrier, inc=1, device_id={"mp": model_peer(off)}, device_id_type=MESH
        )

    for copy in loads.values():
        copy.start()
    target = band_ref[...]
    onehot = jnp.where(
        lax.broadcasted_iota(jnp.int32, (bands, observed), 0) == target, 1.0, 0.0
    )
    before = jnp.where(
        lax.broadcasted_iota(jnp.int32, (observed, observed), 0)
        < lax.broadcasted_iota(jnp.int32, (observed, observed), 1),
        1.0,
        0.0,
    ).astype(low)
    earlier = dot_wide(onehot.astype(low), before)
    rank = jnp.sum(earlier * onehot, axis=0, keepdims=True)
    slot_row = target * capacity + rank.astype(jnp.int32)
    place = jnp.where(
        lax.broadcasted_iota(jnp.int32, (slots, observed), 0) == slot_row, 1.0, 0.0
    ).astype(low)
    loads["observed"].wait()
    row_send[...] = (
        dot_wide(place, observed_ref[:, my_columns]).astype(low).reshape(bands, capacity, columns)
    )
    cell_hot = jnp.where(
        lax.broadcasted_iota(jnp.int32, (blocks, observed), 0) == (cell_ref[...] >> 7), 1.0, 0.0
    ).astype(low)
    cell_hot = jnp.concatenate([cell_hot, jnp.zeros((16 - blocks, observed), low)], axis=0)
    hot = dot_transposed(cell_hot, place).astype(low)
    for s in range(bands):
        hot_send[s] = hot[:, s * capacity : (s + 1) * capacity]

    def incoming(kind, off, source, landing):
        return pltpu.make_async_remote_copy(
            src_ref=source,
            dst_ref=landing,
            send_sem=in_send.at[kind, off],
            recv_sem=in_recv.at[kind, off],
            device_id={"band": band_peer(off)},
            device_id_type=MESH,
        )

    def start_in(kind, source, landing):
        for off in range(1, bands):
            incoming(kind, off, source.at[band_peer(off)], landing.at[me]).start()

    def wait_in(kind, source, landing):
        for off in range(1, bands):
            incoming(kind, off, source.at[band_peer(off)], landing.at[band_source(off)]).wait()

    def arrived(off):
        return incoming(0, off, row_send.at[band_peer(off)], row_got.at[mine, band_source(off)])

    def forward(off, hop, owner):
        block = row_got.at[owner, band_source(off)]
        return pltpu.make_async_remote_copy(
            src_ref=block,
            dst_ref=block,
            send_sem=row_send_sem.at[hop - 1, off],
            recv_sem=row_recv_sem.at[hop - 1, off],
            device_id={"mp": model_peer(hop)},
            device_id_type=MESH,
        )

    def adjoint_rows(q):
        return adjoint_ref.at[pl.ds(pl.multiple_of(q * group, group), group), my_columns]

    row_got[mine, me] = row_send[me]
    loads["adjoint"].wait()
    loads["wo"].wait()
    grad_send[...] = (
        dot_transposed(adjoint_ref[...], wo_ref[...]).astype(low).reshape(bands, group, columns)
    )
    hot_got[me] = hot_send[me]
    grad_got[me] = grad_send[me]
    adj_got[me] = adjoint_ref[pl.ds(pl.multiple_of(me * group, group), group), my_columns]
    for name in ("latents", "wq", "wk", "wv"):
        loads[name].wait()
    queries = (dot_wide(latents_ref[...], wq_ref[...]) * factor).astype(low)
    query_s[...] = queries
    turned = jnp.transpose(queries)
    for t in range(tiles):
        query_t[t] = turned[:, t * TILE : (t + 1) * TILE]
    skey_s[...] = dot_wide(latents_ref[...], wk_ref[...]).astype(low)
    svalue_s[...] = dot_wide(latents_ref[...], wv_ref[...]).astype(low)
    dkey_t[...] = jnp.zeros_like(dkey_t)
    dvalue_t[...] = jnp.zeros_like(dvalue_t)
    lane_head = lax.broadcasted_iota(jnp.int32, (1, columns), 1) // HEAD_DIM
    permute_s[...] = jnp.where(
        lax.broadcasted_iota(jnp.int32, (nodes, nodes), 1) == column_of(map_ref[...]), 1.0, 0.0
    ).astype(low)
    gather_s[...] = jnp.where(
        lax.broadcasted_iota(jnp.int32, (observed, slots), 1) == column_of(slot_row), 1.0, 0.0
    ).astype(low)
    own_s[...] = query_s[...].astype(jnp.float32) * skey_s[...].astype(jnp.float32)
    pl.semaphore_wait(barrier, bands + models - 2)
    start_in(0, row_send, row_got.at[mine])
    start_in(1, hot_send, hot_got)
    for hop in range(1, models):
        forward(0, hop, mine).start()
    start_in(2, grad_send, grad_got)
    for off in range(1, bands):
        incoming(3, off, adjoint_rows(band_peer(off)), adj_got.at[me]).start()

    def pass_on(off):
        arrived(off).wait_recv()
        for hop in range(1, models):
            forward(off, hop, mine).start()

    for off in range(1, bands):
        pass_on(off)

    def split_heads(weights, kept):
        whole = jnp.zeros((slots, columns), jnp.float32)
        for j in range(models):
            whole = whole + dot_wide(
                row_got[j].reshape(slots, columns), weights[j * columns : (j + 1) * columns, :]
            )
        whole = whole.astype(low).astype(jnp.float32)
        for h in range(heads):
            kept[h] = jnp.where(lane_head == h, whole, 0.0).astype(low)

    wait_in(1, hot_send, hot_got)
    hot_all = jnp.concatenate([hot_got[s] for s in range(bands)], axis=1)
    mask = jnp.concatenate(
        [mask_ref[...].astype(jnp.float32), jnp.zeros((blocks, 16 - blocks), jnp.float32)], axis=1
    ).astype(low)
    bias = jnp.where(dot_wide(mask, hot_all) > 0.5, 0.0, -1e30)
    for b in range(blocks):
        bias_s[b] = bias[b : b + 1, :]
    for off in range(bands):
        for hop in range(1, models):
            forward(off, hop, model_source(hop)).wait_recv()
    split_heads(wk_ref, key_heads)
    split_heads(wv_ref, value_heads)
    wait_in(2, grad_send, grad_got)
    grads = dot_wide(permute_s[...], grad_got[...].reshape(nodes, columns)).astype(low)
    grad_s[...] = grads
    turned = jnp.transpose(grads)
    for t in range(tiles):
        grad_t[t] = turned[:, t * TILE : (t + 1) * TILE]

    def back(part, which, off, source_band, landing_band):
        rows = pl.ds(which * columns + part * span, span)
        return pltpu.make_async_remote_copy(
            src_ref=back_send.at[source_band, rows],
            dst_ref=back_got.at[landing_band, rows],
            send_sem=back_send_sem.at[part * 2 + which, off],
            recv_sem=back_recv_sem.at[part * 2 + which, off],
            device_id={"band": band_peer(off)},
            device_id_type=MESH,
        )

    def pair_copy(source, landing, index):
        return pltpu.make_async_remote_copy(
            src_ref=source,
            dst_ref=landing,
            send_sem=pair_send_sem.at[index],
            recv_sem=pair_recv_sem.at[index],
            device_id={"mp": partner},
            device_id_type=MESH,
        )

    def cross_copy(off, source, landing, index):
        return pltpu.make_async_remote_copy(
            src_ref=source,
            dst_ref=landing,
            send_sem=node_send_sem.at[off - 1, index],
            recv_sem=node_recv_sem.at[off - 1, index],
            device_id={"mp": chip_peer(off) * 2 + side},
            device_id_type=MESH,
        )

    def node_exchange(t):
        return pair_copy(node_send.at[1 - side, t], node_pair.at[t], t)

    def node_cross(off, t):
        return cross_copy(off, node_sum.at[off - 1, t], node_got.at[off - 1, t], t)

    def obs_exchange():
        return pair_copy(obs_send.at[1 - side], obs_pair, tiles)

    def obs_cross(off):
        return cross_copy(off, obs_sum.at[off - 1], obs_got.at[off - 1], tiles)

    def node_reduce(t):
        node_exchange(t).wait()
        for off in range(1, chips):
            c = chip_peer(off)
            node_sum[off - 1, t] = (
                node_send[side, t, c].astype(jnp.float32) + node_pair[t, c].astype(jnp.float32)
            ).astype(low)
            node_cross(off, t).start()

    for part in range(passes):

        def tile_step(t, part=part):
            rows = pl.ds(pl.multiple_of(t * TILE, TILE), TILE)
            query = query_s[rows, :]
            grad = grad_s[rows, :]
            grad_wide = grad.astype(jnp.float32)
            svalue_wide = svalue_s[rows, :].astype(jnp.float32)
            own_products = own_s[rows, :]
            own_dproducts = grad_wide * svalue_wide
            penalty = bias_s[pl.ds(t * per_tile, per_tile)]
            if part == 0:
                own_dscores = jnp.zeros((TILE, columns), jnp.float32)
                own_probs = jnp.zeros((TILE, columns), jnp.float32)
            else:
                own_dscores = dscore_s[rows, :]
                own_probs = prob_s[rows, :]
            for h in range(part * HEADS_PER_PASS, (part + 1) * HEADS_PER_PASS):
                lanes = lane_head == h
                keys = key_heads[h]
                scores = dot_transposed(query, keys)
                scores = (scores.reshape(per_tile, BLOCK, slots) + penalty).reshape(TILE, slots)
                own_score = jnp.sum(jnp.where(lanes, own_products, 0.0), axis=1, keepdims=True)
                own_dprob = jnp.sum(jnp.where(lanes, own_dproducts, 0.0), axis=1, keepdims=True)
                highest = jnp.maximum(jnp.max(scores, axis=1, keepdims=True), own_score)
                weights = jnp.exp(scores - highest)
                own_weight = jnp.exp(own_score - highest)
                inverse = 1.0 / (jnp.sum(weights, axis=1, keepdims=True) + own_weight)
                probs = weights * inverse
                own_prob = own_weight * inverse
                dprobs = dot_transposed(grad, value_heads[h])
                centre = jnp.sum(probs * dprobs, axis=1, keepdims=True) + own_prob * own_dprob
                dscore_low = (probs * (dprobs - centre)).astype(low)
                probs_low = probs.astype(low)
                own_dscore = own_prob * (own_dprob - centre)
                dscore_low_s[h, rows, :] = dscore_low
                own_dscores = jnp.where(lanes, own_dscore, own_dscores)
                own_probs = jnp.where(lanes, own_prob, own_probs)
                features = pl.ds(h * HEAD_DIM, HEAD_DIM)
                dkey_t[features, :] += dot_wide(query_t[t, features, :], dscore_low)
                dvalue_t[features, :] += dot_wide(grad_t[t, features, :], probs_low)
            dscore_s[rows, :] = own_dscores
            prob_s[rows, :] = own_probs

        def some_tiles(i, carry):
            for u in range(UNROLL):
                tile_step(i * UNROLL + u)
            return carry

        lax.fori_loop(0, tiles // UNROLL, some_tiles, 0)
        for which, total in ((0, dkey_t), (1, dvalue_t)):
            done = total[pl.ds(part * span, span), :].astype(low)
            for s in range(bands):
                back_send[s, pl.ds(which * columns + part * span, span), :] = done[
                    :, s * capacity : (s + 1) * capacity
                ]
            for off in range(1, bands):
                back(part, which, off, band_peer(off), me).start()
    back_got[me] = back_send[me]

    weights_all = jnp.concatenate([wq_ref[...], wk_ref[...], wv_ref[...]], axis=1)
    for t in range(tiles):
        rows = slice(t * TILE, (t + 1) * TILE)
        dquery = dot_wide(dscore_low_s[0, rows, :], key_heads[0])
        for h in range(1, heads):
            dquery = dquery + dot_wide(dscore_low_s[h, rows, :], key_heads[h])
        own_dscores = dscore_s[rows, :]
        pieces = jnp.concatenate(
            [
                ((dquery + own_dscores * skey_s[rows, :].astype(jnp.float32)) * factor).astype(low),
                (own_dscores * query_s[rows, :].astype(jnp.float32)).astype(low),
                (prob_s[rows, :] * grad_s[rows, :].astype(jnp.float32)).astype(low),
            ],
            axis=1,
        )
        term = dot_transposed(pieces, weights_all).astype(low)
        for j in range(models):
            node_send[j % 2, t, j // 2] = term[:, j * columns : (j + 1) * columns]
        node_exchange(t).start()
        if t:
            node_reduce(t - 1)
    for off in range(1, bands):
        incoming(3, off, adjoint_rows(band_peer(off)), adj_got.at[band_source(off)]).wait()
    adjoint_mine = dot_wide(permute_s[...], adj_got[...].reshape(nodes, columns))
    node_reduce(tiles - 1)
    for part in range(passes):
        for which in range(2):
            for off in range(1, bands):
                back(part, which, off, band_peer(off), band_source(off)).wait()
    returned = jnp.concatenate([back_got[s] for s in range(bands)], axis=1)
    own_pairs = dot_transposed(gather_s[...], returned).astype(low)
    w_pair = jnp.concatenate([wk_ref[...], wv_ref[...]], axis=1)
    obs_term = dot_transposed(own_pairs, w_pair).astype(low)
    for j in range(models):
        obs_send[j % 2, j // 2] = obs_term[:, j * columns : (j + 1) * columns]
    obs_exchange().start()
    obs_exchange().wait()
    for off in range(1, chips):
        c = chip_peer(off)
        obs_sum[off - 1] = (
            obs_send[side, c].astype(jnp.float32) + obs_pair[c].astype(jnp.float32)
        ).astype(low)
        obs_cross(off).start()
    for t in range(tiles):
        rows = slice(t * TILE, (t + 1) * TILE)
        total = node_send[side, t, chip].astype(jnp.float32)
        total = total + node_pair[t, chip].astype(jnp.float32)
        for off in range(1, chips):
            node_cross(off, t).wait()
            total = total + node_got[off - 1, t].astype(jnp.float32)
        node_out[rows, :] = (adjoint_mine[rows, :] + total).astype(low)
    for off in range(1, bands):
        arrived(off).wait_send()
    for off in range(bands):
        for hop in range(1, models):
            forward(off, hop, mine).wait_send()
    total = obs_send[side, chip].astype(jnp.float32) + obs_pair[chip].astype(jnp.float32)
    for off in range(1, chips):
        obs_cross(off).wait()
        total = total + obs_got[off - 1].astype(jnp.float32)
    observed_out[...] = total.astype(low)


def write_kernel(node_ref, observed_ref, node_out, observed_out):
    node_out[...] = node_ref[...]
    observed_out[...] = observed_ref[...]


def on_device(
    node_adjoint,
    band_map,
    latents,
    observations,
    route_band,
    route_cell,
    block_mask,
    w_query,
    w_key,
    w_value,
    w_out,
):
    bands = lax.axis_size("band")
    models = lax.axis_size("mp")
    chips = models // 2
    nodes = latents.shape[0]
    columns = w_query.shape[1]
    heads = columns // HEAD_DIM
    observed = observations.shape[0]
    capacity = 2 * observed // bands
    slots = capacity * bands
    group = nodes // bands
    blocks = block_mask.shape[1]
    tiles = nodes // TILE
    passes = heads // HEADS_PER_PASS
    low, wide = jnp.bfloat16, jnp.float32
    dma = pltpu.SemaphoreType.DMA
    vmem = pl.BlockSpec(memory_space=pltpu.VMEM)
    far = pl.BlockSpec(memory_space=pl.ANY)
    grads = pl.pallas_call(
        functools.partial(encoder_kernel, bands, models),
        out_shape=(
            jax.ShapeDtypeStruct((nodes, columns), low),
            jax.ShapeDtypeStruct((observed, columns), low),
        ),
        in_specs=[far, vmem, far, far, vmem, vmem, vmem, far, far, far, far],
        out_specs=(vmem, vmem),
        scratch_shapes=[
            pltpu.VMEM(node_adjoint.shape, low),
            pltpu.VMEM(latents.shape, low),
            pltpu.VMEM(observations.shape, low),
            pltpu.VMEM(w_query.shape, low),
            pltpu.VMEM(w_key.shape, low),
            pltpu.VMEM(w_value.shape, low),
            pltpu.VMEM(w_out.shape, low),
            dma((7,)),
            pltpu.VMEM((bands, capacity, columns), low),
            pltpu.VMEM((bands, 16, capacity), low),
            pltpu.VMEM((bands, group, columns), low),
            pltpu.VMEM((models, bands, capacity, columns), low),
            pltpu.VMEM((bands, 16, capacity), low),
            pltpu.VMEM((bands, group, columns), low),
            pltpu.VMEM((bands, group, columns), low),
            pltpu.VMEM((nodes, columns), low),
            pltpu.VMEM((tiles, columns, TILE), low),
            pltpu.VMEM((nodes, columns), low),
            pltpu.VMEM((nodes, columns), low),
            pltpu.VMEM((nodes, columns), low),
            pltpu.VMEM((tiles, columns, TILE), low),
            pltpu.VMEM((heads, slots, columns), low),
            pltpu.VMEM((heads, slots, columns), low),
            pltpu.VMEM((blocks, 1, slots), wide),
            pltpu.VMEM((columns, slots), wide),
            pltpu.VMEM((columns, slots), wide),
            pltpu.VMEM((heads, nodes, slots), low),
            pltpu.VMEM((nodes, columns), wide),
            pltpu.VMEM((nodes, columns), wide),
            pltpu.VMEM((nodes, nodes), low),
            pltpu.VMEM((observed, slots), low),
            pltpu.VMEM((nodes, columns), wide),
            pltpu.VMEM((bands, 2 * columns, capacity), low),
            pltpu.VMEM((bands, 2 * columns, capacity), low),
            pltpu.VMEM((2, tiles, chips, TILE, columns), low),
            pltpu.VMEM((tiles, chips, TILE, columns), low),
            pltpu.VMEM((chips - 1, tiles, TILE, columns), low),
            pltpu.VMEM((chips - 1, tiles, TILE, columns), low),
            pltpu.VMEM((2, chips, observed, columns), low),
            pltpu.VMEM((chips, observed, columns), low),
            pltpu.VMEM((chips - 1, observed, columns), low),
            pltpu.VMEM((chips - 1, observed, columns), low),
            dma((4, bands)),
            dma((4, bands)),
            dma((models - 1, bands)),
            dma((models - 1, bands)),
            dma((2 * passes, bands)),
            dma((2 * passes, bands)),
            dma((chips - 1, tiles + 1)),
            dma((chips - 1, tiles + 1)),
            dma((tiles + 1,)),
            dma((tiles + 1,)),
        ],
        compiler_params=pltpu.CompilerParams(collective_id=0, has_side_effects=True),
    )(
        node_adjoint,
        band_map,
        latents,
        observations,
        route_band.reshape(1, observed),
        route_cell.reshape(1, observed),
        block_mask,
        w_query,
        w_key,
        w_value,
        w_out,
    )
    return pl.pallas_call(
        write_kernel,
        out_shape=tuple(jax.ShapeDtypeStruct(g.shape, g.dtype) for g in grads),
        in_specs=(vmem, vmem),
        out_specs=(vmem, vmem),
    )(*grads)


def solution(mesh):
    bands = mesh.shape["band"]

    def body(*arrays):
        capacity = 2 * arrays[3].shape[0] // bands
        group = arrays[0].shape[0] // bands
        tiled = capacity % 128 == 0 and group % 16 == 0
        return (on_device if tiled else on_device_plain)(*arrays)

    return jax.shard_map(
        body,
        mesh=mesh,
        in_specs=(
            P("band", None),
            P("band", None),
            P("band", None),
            P("band", None),
            P("band", None),
            P("band"),
            P("band", None),
            P(None, "mp"),
            P(None, "mp"),
            P(None, "mp"),
            P("mp", None),
        ),
        out_specs=(P("band", "mp"), P("band", "mp")),
        check_vma=False,
    )
```

```python
import functools
import math

import jax
import jax.numpy as jnp
from jax import lax
from jax.experimental import pallas as pl
from jax.experimental.pallas import tpu as pltpu
from jax.sharding import PartitionSpec as P

HEAD_DIM = 32
BLOCK = 128


def dot_wide(left, right):
    return jnp.dot(left, right, preferred_element_type=jnp.float32)


def dot_transposed(left, right):
    return lax.dot_general(
        left, right, (((1,), (1,)), ((), ())), preferred_element_type=jnp.float32
    )


def broaden_precision(value):
    return lax.optimization_barrier(value).astype(jnp.float32)


def send_slots(route_band, band_count, capacity):
    target = route_band[:, 0]
    onehot = (target[:, None] == jnp.arange(band_count, dtype=jnp.int32)[None, :]).astype(jnp.int32)
    earlier = jnp.cumsum(onehot, axis=0) - onehot
    rank_within = jnp.sum(earlier * onehot, axis=1)
    return target * capacity + rank_within


def on_device_plain(
    node_adjoint,
    band_map,
    latents,
    observations,
    route_band,
    route_cell,
    block_mask,
    w_query,
    w_key,
    w_value,
    w_out,
):
    band_count = lax.axis_size("band")
    node_count = latents.shape[0]
    column_count = w_query.shape[1]
    head_count = column_count // HEAD_DIM
    observed_rows = observations.shape[0]
    capacity = 2 * observed_rows // band_count
    slot_count = capacity * band_count
    block_count = block_mask.shape[1]
    model_index = lax.axis_index("mp")
    score_factor_scale = 1.0 / math.sqrt(HEAD_DIM)
    w_pair = jnp.concatenate([w_key, w_value], axis=1)
    arrival = band_map[0]
    received = lax.all_to_all(node_adjoint, "band", split_axis=0, concat_axis=0, tiled=True)
    adjoint = jnp.take(received, arrival, axis=0)
    adjoint_part = lax.dynamic_slice_in_dim(adjoint, model_index * column_count, column_count, 1)
    target_slot = send_slots(route_band, band_count, capacity)
    cell_send = jnp.full((slot_count,), -1, jnp.int32).at[target_slot].set(route_cell)
    own_rows = lax.dynamic_slice_in_dim(observations, model_index * column_count, column_count, 1)
    row_send = jnp.zeros((slot_count, column_count), jnp.bfloat16).at[target_slot].set(own_rows)
    row_arrived, slot_cells = (
        lax.all_to_all(row_send, "band", split_axis=0, concat_axis=0, tiled=True),
        lax.all_to_all(cell_send, "band", split_axis=0, concat_axis=0, tiled=True),
    )
    full_rows = lax.all_gather(row_arrived, "mp", axis=1, tiled=True)
    key_pairs = dot_wide(full_rows, w_pair).astype(jnp.bfloat16)
    key_head_split = key_pairs[:, :column_count].reshape(slot_count, head_count, HEAD_DIM)
    value_heads = key_pairs[:, column_count:].reshape(slot_count, head_count, HEAD_DIM)
    key_hot = (
        (slot_cells // BLOCK)[:, None] == jnp.arange(block_count, dtype=jnp.int32)[None, :]
    ).astype(jnp.bfloat16)
    node_mask = jnp.repeat(block_mask, BLOCK, axis=0).astype(jnp.bfloat16)
    queries = (dot_wide(latents, w_query) * score_factor_scale).astype(jnp.bfloat16)
    self_pair = dot_wide(latents, w_pair).astype(jnp.bfloat16)
    self_pair_key = self_pair[:, :column_count]
    self_value = self_pair[:, column_count:]
    grad_out = dot_transposed(adjoint, w_out).astype(jnp.bfloat16)
    block_rows = min(512, node_count)
    block_total = node_count // block_rows

    def split_blocks(value):
        return value.reshape(block_total, block_rows, head_count, HEAD_DIM)

    stacked = (
        split_blocks(queries),
        split_blocks(self_pair_key),
        split_blocks(self_value),
        split_blocks(grad_out),
        node_mask.reshape(block_total, block_rows, block_count),
    )

    def attend(running, block_entries):
        key_grad, value_grad = running
        query_tile, self_key_tile, self_value_tile, gradient_block, block_mask_tile = block_entries
        scores = jnp.einsum(
            "qhd,khd->hqk", query_tile, key_head_split, preferred_element_type=jnp.float32
        )
        allowed = (dot_transposed(block_mask_tile, key_hot) > 0.5)[None]
        query_widened = broaden_precision(query_tile)
        grad_wide = broaden_precision(gradient_block)
        self_key_widened = broaden_precision(self_key_tile)
        self_score = jnp.transpose(jnp.sum(query_widened * self_key_widened, axis=2))
        highest = jnp.maximum(jnp.max(jnp.where(allowed, scores, -jnp.inf), axis=2), self_score)
        weights = jnp.where(allowed, jnp.exp(scores - highest[:, :, None]), 0.0)
        own_weight = jnp.exp(self_score - highest)
        normaliser = jnp.sum(weights, axis=2) + own_weight
        probabilities = weights / normaliser[:, :, None]
        own_prob = own_weight / normaliser
        probabilities_low = probabilities.astype(jnp.bfloat16)
        dprobs = jnp.einsum(
            "qhd,khd->hqk", gradient_block, value_heads, preferred_element_type=jnp.float32
        )
        own_dprob = jnp.transpose(jnp.sum(grad_wide * broaden_precision(self_value_tile), axis=2))
        centre = jnp.sum(probabilities * dprobs, axis=2) + own_prob * own_dprob
        dscore = probabilities * (dprobs - centre[:, :, None])
        own_dscore = own_prob * (own_dprob - centre)
        score_gradient_narrow = dscore.astype(jnp.bfloat16)
        self_score_gradient_rows = jnp.transpose(own_dscore)[:, :, None]
        own_prob_rows = jnp.transpose(own_prob)[:, :, None]
        query_gradient = jnp.einsum(
            "hqk,khd->qhd",
            score_gradient_narrow,
            key_head_split,
            preferred_element_type=jnp.float32,
        )
        query_gradient = (
            (query_gradient + self_score_gradient_rows * self_key_widened) * score_factor_scale
        ).astype(jnp.bfloat16)
        dself_key = (self_score_gradient_rows * query_widened).astype(jnp.bfloat16)
        dself_value = (own_prob_rows * grad_wide).astype(jnp.bfloat16)
        key_grad = key_grad + jnp.einsum(
            "hqk,qhd->khd", score_gradient_narrow, query_tile, preferred_element_type=jnp.float32
        )
        value_grad = value_grad + jnp.einsum(
            "hqk,qhd->khd", probabilities_low, gradient_block, preferred_element_type=jnp.float32
        )
        flat_shape = (block_rows, column_count)
        node_pieces = jnp.concatenate(
            [
                query_gradient.reshape(flat_shape),
                dself_key.reshape(flat_shape),
                dself_value.reshape(flat_shape),
            ],
            axis=1,
        )
        return ((key_grad, value_grad), node_pieces)

    zero_grads = jnp.zeros((slot_count, head_count, HEAD_DIM), jnp.float32)
    (key_grad, value_grad), node_pieces = lax.scan(attend, (zero_grads, zero_grads), stacked)
    node_pieces = node_pieces.reshape(node_count, 3 * column_count)
    w_triple = jnp.concatenate([w_query, w_key, w_value], axis=1)
    node_term = dot_transposed(node_pieces, w_triple)
    node_sum = lax.psum_scatter(
        node_term.astype(jnp.bfloat16), "mp", scatter_dimension=1, tiled=True
    ).astype(jnp.float32)
    node_grad = (adjoint_part.astype(jnp.float32) + node_sum).astype(jnp.bfloat16)
    grad_pairs = jnp.concatenate(
        [
            key_grad.astype(jnp.bfloat16).reshape(slot_count, column_count),
            value_grad.astype(jnp.bfloat16).reshape(slot_count, column_count),
        ],
        axis=1,
    )
    slot_term = dot_transposed(grad_pairs, w_pair)
    slot_sum = lax.psum_scatter(
        slot_term.astype(jnp.bfloat16), "mp", scatter_dimension=1, tiled=True
    )
    returned = lax.all_to_all(slot_sum, "band", split_axis=0, concat_axis=0, tiled=True)
    observation_grad = jnp.take(returned, target_slot, axis=0)
    return (node_grad, observation_grad)


TILE = 256
HEADS_PER_PASS = 1
UNROLL = 2
MESH = pl.DeviceIdType.MESH


def dot_first(left, right):
    return lax.dot_general(
        left, right, (((0,), (0,)), ((), ())), preferred_element_type=jnp.float32
    )


def column_of(row, rows=128):
    wide = jnp.transpose(jnp.broadcast_to(row.astype(jnp.float32), (rows, row.shape[1])))
    return wide[:, :1].astype(jnp.int32)


def encoder_kernel(
    bands,
    models,
    adjoint_hbm,
    map_ref,
    latents_hbm,
    observed_hbm,
    band_ref,
    cell_ref,
    mask_ref,
    wq_hbm,
    wk_hbm,
    wv_hbm,
    wo_hbm,
    node_out,
    observed_out,
    adjoint_ref,
    latents_ref,
    observed_ref,
    wq_ref,
    wk_ref,
    wv_ref,
    wo_ref,
    load_sem,
    row_send,
    hot_send,
    grad_send,
    row_got,
    hot_got,
    grad_got,
    adj_got,
    query_s,
    query_t,
    skey_s,
    svalue_s,
    grad_s,
    grad_t,
    key_heads,
    value_heads,
    bias_s,
    dkey_t,
    dvalue_t,
    dscore_low_s,
    dscore_s,
    prob_s,
    permute_s,
    gather_s,
    own_s,
    back_send,
    back_got,
    node_send,
    node_pair,
    node_sum,
    node_got,
    obs_send,
    obs_pair,
    obs_sum,
    obs_got,
    in_send,
    in_recv,
    row_send_sem,
    row_recv_sem,
    back_send_sem,
    back_recv_sem,
    node_send_sem,
    node_recv_sem,
    pair_send_sem,
    pair_recv_sem,
):
    me = lax.axis_index("band")
    mine = lax.axis_index("mp")
    nodes = latents_ref.shape[0]
    columns = wq_ref.shape[1]
    heads = columns // HEAD_DIM
    observed = observed_ref.shape[0]
    capacity = row_got.shape[2]
    slots = bands * capacity
    group = grad_got.shape[1]
    blocks = mask_ref.shape[1]
    tiles = nodes // TILE
    per_tile = TILE // BLOCK
    passes = heads // HEADS_PER_PASS
    span = HEADS_PER_PASS * HEAD_DIM
    factor = 1.0 / math.sqrt(HEAD_DIM)
    low = jnp.bfloat16

    def band_peer(off):
        return lax.rem(me + off, bands)

    def band_source(off):
        return lax.rem(me + bands - off, bands)

    def model_peer(off):
        return lax.rem(mine + off, models)

    def model_source(off):
        return lax.rem(mine + models - off, models)

    chips = models // 2
    side = lax.rem(mine, 2)
    chip = mine // 2
    partner = mine + 1 - 2 * side
    my_columns = pl.ds(pl.multiple_of(mine * columns, columns), columns)

    def chip_peer(off):
        return lax.rem(chip + off, chips)

    loads = {}
    for index, (name, source, landing) in enumerate(
        (
            ("observed", observed_hbm, observed_ref),
            ("adjoint", adjoint_hbm, adjoint_ref),
            ("wo", wo_hbm, wo_ref),
            ("latents", latents_hbm, latents_ref),
            ("wq", wq_hbm, wq_ref),
            ("wk", wk_hbm, wk_ref),
            ("wv", wv_hbm, wv_ref),
        )
    ):
        loads[name] = pltpu.make_async_copy(source, landing, load_sem.at[index])

    barrier = pltpu.get_barrier_semaphore()
    for off in range(1, bands):
        pl.semaphore_signal(
            barrier, inc=1, device_id={"band": band_peer(off)}, device_id_type=MESH
        )
    for off in range(1, models):
        pl.semaphore_signal(
            barrier, inc=1, device_id={"mp": model_peer(off)}, device_id_type=MESH
        )

    for copy in loads.values():
        copy.start()
    target = band_ref[...]
    onehot = jnp.where(
        lax.broadcasted_iota(jnp.int32, (bands, observed), 0) == target, 1.0, 0.0
    )
    before = jnp.where(
        lax.broadcasted_iota(jnp.int32, (observed, observed), 0)
        < lax.broadcasted_iota(jnp.int32, (observed, observed), 1),
        1.0,
        0.0,
    ).astype(low)
    earlier = dot_wide(onehot.astype(low), before)
    rank = jnp.sum(earlier * onehot, axis=0, keepdims=True)
    slot_row = target * capacity + rank.astype(jnp.int32)
    place = jnp.where(
        lax.broadcasted_iota(jnp.int32, (slots, observed), 0) == slot_row, 1.0, 0.0
    ).astype(low)
    loads["observed"].wait()
    row_send[...] = (
        dot_wide(place, observed_ref[:, my_columns]).astype(low).reshape(bands, capacity, columns)
    )
    cell_hot = jnp.where(
        lax.broadcasted_iota(jnp.int32, (blocks, observed), 0) == (cell_ref[...] >> 7), 1.0, 0.0
    ).astype(low)
    cell_hot = jnp.concatenate([cell_hot, jnp.zeros((16 - blocks, observed), low)], axis=0)
    hot = dot_transposed(cell_hot, place).astype(low)
    for s in range(bands):
        hot_send[s] = hot[:, s * capacity : (s + 1) * capacity]

    def incoming(kind, off, source, landing):
        return pltpu.make_async_remote_copy(
            src_ref=source,
            dst_ref=landing,
            send_sem=in_send.at[kind, off],
            recv_sem=in_recv.at[kind, off],
            device_id={"band": band_peer(off)},
            device_id_type=MESH,
        )

    def start_in(kind, source, landing):
        for off in range(1, bands):
            incoming(kind, off, source.at[band_peer(off)], landing.at[me]).start()

    def wait_in(kind, source, landing):
        for off in range(1, bands):
            incoming(kind, off, source.at[band_peer(off)], landing.at[band_source(off)]).wait()

    def arrived(off):
        return incoming(0, off, row_send.at[band_peer(off)], row_got.at[mine, band_source(off)])

    def forward(off, hop, owner):
        block = row_got.at[owner, band_source(off)]
        return pltpu.make_async_remote_copy(
            src_ref=block,
            dst_ref=block,
            send_sem=row_send_sem.at[hop - 1, off],
            recv_sem=row_recv_sem.at[hop - 1, off],
            device_id={"mp": model_peer(hop)},
            device_id_type=MESH,
        )

    def adjoint_rows(q):
        return adjoint_ref.at[pl.ds(pl.multiple_of(q * group, group), group), my_columns]

    row_got[mine, me] = row_send[me]
    loads["adjoint"].wait()
    loads["wo"].wait()
    grad_send[...] = (
        dot_transposed(adjoint_ref[...], wo_ref[...]).astype(low).reshape(bands, group, columns)
    )
    hot_got[me] = hot_send[me]
    grad_got[me] = grad_send[me]
    adj_got[me] = adjoint_ref[pl.ds(pl.multiple_of(me * group, group), group), my_columns]
    pl.semaphore_wait(barrier, bands + models - 2)
    start_in(0, row_send, row_got.at[mine])
    start_in(1, hot_send, hot_got)
    for hop in range(1, models):
        forward(0, hop, mine).start()
    start_in(2, grad_send, grad_got)
    for off in range(1, bands):
        incoming(3, off, adjoint_rows(band_peer(off)), adj_got.at[me]).start()

    def pass_on(off):
        arrived(off).wait_recv()
        for hop in range(1, models):
            forward(off, hop, mine).start()

    for name in ("latents", "wq", "wk", "wv"):
        loads[name].wait()
    queries = (dot_wide(latents_ref[...], wq_ref[...]) * factor).astype(low)
    query_s[...] = queries
    turned = jnp.transpose(queries)
    for t in range(tiles):
        query_t[t] = turned[:, t * TILE : (t + 1) * TILE]
    for off in range(1, bands // 2):
        pass_on(off)
    skey_s[...] = dot_wide(latents_ref[...], wk_ref[...]).astype(low)
    svalue_s[...] = dot_wide(latents_ref[...], wv_ref[...]).astype(low)
    dkey_t[...] = jnp.zeros_like(dkey_t)
    dvalue_t[...] = jnp.zeros_like(dvalue_t)
    lane_head = lax.broadcasted_iota(jnp.int32, (1, columns), 1) // HEAD_DIM
    for off in range(bands // 2, bands):
        pass_on(off)
    permute_s[...] = jnp.where(
        lax.broadcasted_iota(jnp.int32, (nodes, nodes), 1) == column_of(map_ref[...]), 1.0, 0.0
    ).astype(low)
    gather_s[...] = jnp.where(
        lax.broadcasted_iota(jnp.int32, (observed, slots), 1) == column_of(slot_row), 1.0, 0.0
    ).astype(low)
    own_s[...] = query_s[...].astype(jnp.float32) * skey_s[...].astype(jnp.float32)

    def split_heads(weights, kept):
        whole = jnp.zeros((slots, columns), jnp.float32)
        for j in range(models):
            whole = whole + dot_wide(
                row_got[j].reshape(slots, columns), weights[j * columns : (j + 1) * columns, :]
            )
        whole = whole.astype(low).astype(jnp.float32)
        for h in range(heads):
            kept[h] = jnp.where(lane_head == h, whole, 0.0).astype(low)

    wait_in(1, hot_send, hot_got)
    hot_all = jnp.concatenate([hot_got[s] for s in range(bands)], axis=1)
    mask = jnp.concatenate(
        [mask_ref[...].astype(jnp.float32), jnp.zeros((blocks, 16 - blocks), jnp.float32)], axis=1
    ).astype(low)
    bias = jnp.where(dot_wide(mask, hot_all) > 0.5, 0.0, -1e30)
    for b in range(blocks):
        bias_s[b] = bias[b : b + 1, :]
    for off in range(bands):
        for hop in range(1, models):
            forward(off, hop, model_source(hop)).wait_recv()
    split_heads(wk_ref, key_heads)
    split_heads(wv_ref, value_heads)
    wait_in(2, grad_send, grad_got)
    grads = dot_wide(permute_s[...], grad_got[...].reshape(nodes, columns)).astype(low)
    grad_s[...] = grads
    turned = jnp.transpose(grads)
    for t in range(tiles):
        grad_t[t] = turned[:, t * TILE : (t + 1) * TILE]

    def back(part, which, off, source_band, landing_band):
        rows = pl.ds(which * columns + part * span, span)
        return pltpu.make_async_remote_copy(
            src_ref=back_send.at[source_band, rows],
            dst_ref=back_got.at[landing_band, rows],
            send_sem=back_send_sem.at[part * 2 + which, off],
            recv_sem=back_recv_sem.at[part * 2 + which, off],
            device_id={"band": band_peer(off)},
            device_id_type=MESH,
        )

    def pair_copy(source, landing, index):
        return pltpu.make_async_remote_copy(
            src_ref=source,
            dst_ref=landing,
            send_sem=pair_send_sem.at[index],
            recv_sem=pair_recv_sem.at[index],
            device_id={"mp": partner},
            device_id_type=MESH,
        )

    def cross_copy(off, source, landing, index):
        return pltpu.make_async_remote_copy(
            src_ref=source,
            dst_ref=landing,
            send_sem=node_send_sem.at[off - 1, index],
            recv_sem=node_recv_sem.at[off - 1, index],
            device_id={"mp": chip_peer(off) * 2 + side},
            device_id_type=MESH,
        )

    def node_exchange(t):
        return pair_copy(node_send.at[1 - side, t], node_pair.at[t], t)

    def node_cross(off, t):
        return cross_copy(off, node_sum.at[off - 1, t], node_got.at[off - 1, t], t)

    def obs_exchange():
        return pair_copy(obs_send.at[1 - side], obs_pair, tiles)

    def obs_cross(off):
        return cross_copy(off, obs_sum.at[off - 1], obs_got.at[off - 1], tiles)

    def node_reduce(t):
        node_exchange(t).wait()
        for off in range(1, chips):
            c = chip_peer(off)
            node_sum[off - 1, t] = (
                node_send[side, t, c].astype(jnp.float32) + node_pair[t, c].astype(jnp.float32)
            ).astype(low)
            node_cross(off, t).start()

    for part in range(passes):

        def tile_step(t, part=part):
            rows = pl.ds(pl.multiple_of(t * TILE, TILE), TILE)
            query = query_s[rows, :]
            grad = grad_s[rows, :]
            grad_wide = grad.astype(jnp.float32)
            svalue_wide = svalue_s[rows, :].astype(jnp.float32)
            own_products = own_s[rows, :]
            own_dproducts = grad_wide * svalue_wide
            penalty = bias_s[pl.ds(t * per_tile, per_tile)]
            if part == 0:
                own_dscores = jnp.zeros((TILE, columns), jnp.float32)
                own_probs = jnp.zeros((TILE, columns), jnp.float32)
            else:
                own_dscores = dscore_s[rows, :]
                own_probs = prob_s[rows, :]
            for h in range(part * HEADS_PER_PASS, (part + 1) * HEADS_PER_PASS):
                lanes = lane_head == h
                keys = key_heads[h]
                scores = dot_transposed(query, keys)
                scores = (scores.reshape(per_tile, BLOCK, slots) + penalty).reshape(TILE, slots)
                own_score = jnp.sum(jnp.where(lanes, own_products, 0.0), axis=1, keepdims=True)
                own_dprob = jnp.sum(jnp.where(lanes, own_dproducts, 0.0), axis=1, keepdims=True)
                highest = jnp.maximum(jnp.max(scores, axis=1, keepdims=True), own_score)
                weights = jnp.exp(scores - highest)
                own_weight = jnp.exp(own_score - highest)
                inverse = 1.0 / (jnp.sum(weights, axis=1, keepdims=True) + own_weight)
                probs = weights * inverse
                own_prob = own_weight * inverse
                dprobs = dot_transposed(grad, value_heads[h])
                centre = jnp.sum(probs * dprobs, axis=1, keepdims=True) + own_prob * own_dprob
                dscore_low = (probs * (dprobs - centre)).astype(low)
                probs_low = probs.astype(low)
                own_dscore = own_prob * (own_dprob - centre)
                dscore_low_s[h, rows, :] = dscore_low
                own_dscores = jnp.where(lanes, own_dscore, own_dscores)
                own_probs = jnp.where(lanes, own_prob, own_probs)
                features = pl.ds(h * HEAD_DIM, HEAD_DIM)
                dkey_t[features, :] += dot_wide(query_t[t, features, :], dscore_low)
                dvalue_t[features, :] += dot_wide(grad_t[t, features, :], probs_low)
            dscore_s[rows, :] = own_dscores
            prob_s[rows, :] = own_probs

        def some_tiles(i, carry):
            for u in range(UNROLL):
                tile_step(i * UNROLL + u)
            return carry

        lax.fori_loop(0, tiles // UNROLL, some_tiles, 0)
        for which, total in ((0, dkey_t), (1, dvalue_t)):
            done = total[pl.ds(part * span, span), :].astype(low)
            for s in range(bands):
                back_send[s, pl.ds(which * columns + part * span, span), :] = done[
                    :, s * capacity : (s + 1) * capacity
                ]
            for off in range(1, bands):
                back(part, which, off, band_peer(off), me).start()
    back_got[me] = back_send[me]

    weights_all = jnp.concatenate([wq_ref[...], wk_ref[...], wv_ref[...]], axis=1)
    for t in range(tiles):
        rows = slice(t * TILE, (t + 1) * TILE)
        dquery = dot_wide(dscore_low_s[0, rows, :], key_heads[0])
        for h in range(1, heads):
            dquery = dquery + dot_wide(dscore_low_s[h, rows, :], key_heads[h])
        own_dscores = dscore_s[rows, :]
        pieces = jnp.concatenate(
            [
                ((dquery + own_dscores * skey_s[rows, :].astype(jnp.float32)) * factor).astype(low),
                (own_dscores * query_s[rows, :].astype(jnp.float32)).astype(low),
                (prob_s[rows, :] * grad_s[rows, :].astype(jnp.float32)).astype(low),
            ],
            axis=1,
        )
        term = dot_transposed(pieces, weights_all).astype(low)
        for j in range(models):
            node_send[j % 2, t, j // 2] = term[:, j * columns : (j + 1) * columns]
        node_exchange(t).start()
        if t:
            node_reduce(t - 1)
    for off in range(1, bands):
        incoming(3, off, adjoint_rows(band_peer(off)), adj_got.at[band_source(off)]).wait()
    adjoint_mine = dot_wide(permute_s[...], adj_got[...].reshape(nodes, columns))
    node_reduce(tiles - 1)
    for part in range(passes):
        for which in range(2):
            for off in range(1, bands):
                back(part, which, off, band_peer(off), band_source(off)).wait()
    returned = jnp.concatenate([back_got[s] for s in range(bands)], axis=1)
    own_pairs = dot_transposed(gather_s[...], returned).astype(low)
    w_pair = jnp.concatenate([wk_ref[...], wv_ref[...]], axis=1)
    obs_term = dot_transposed(own_pairs, w_pair).astype(low)
    for j in range(models):
        obs_send[j % 2, j // 2] = obs_term[:, j * columns : (j + 1) * columns]
    obs_exchange().start()
    obs_exchange().wait()
    for off in range(1, chips):
        c = chip_peer(off)
        obs_sum[off - 1] = (
            obs_send[side, c].astype(jnp.float32) + obs_pair[c].astype(jnp.float32)
        ).astype(low)
        obs_cross(off).start()
    for t in range(tiles):
        rows = slice(t * TILE, (t + 1) * TILE)
        total = node_send[side, t, chip].astype(jnp.float32)
        total = total + node_pair[t, chip].astype(jnp.float32)
        for off in range(1, chips):
            node_cross(off, t).wait()
            total = total + node_got[off - 1, t].astype(jnp.float32)
        node_out[rows, :] = (adjoint_mine[rows, :] + total).astype(low)
    for off in range(1, bands):
        arrived(off).wait_send()
    for off in range(bands):
        for hop in range(1, models):
            forward(off, hop, mine).wait_send()
    total = obs_send[side, chip].astype(jnp.float32) + obs_pair[chip].astype(jnp.float32)
    for off in range(1, chips):
        obs_cross(off).wait()
        total = total + obs_got[off - 1].astype(jnp.float32)
    observed_out[...] = total.astype(low)


def write_kernel(node_ref, observed_ref, node_out, observed_out):
    node_out[...] = node_ref[...]
    observed_out[...] = observed_ref[...]


def on_device(
    node_adjoint,
    band_map,
    latents,
    observations,
    route_band,
    route_cell,
    block_mask,
    w_query,
    w_key,
    w_value,
    w_out,
):
    bands = lax.axis_size("band")
    models = lax.axis_size("mp")
    chips = models // 2
    nodes = latents.shape[0]
    columns = w_query.shape[1]
    heads = columns // HEAD_DIM
    observed = observations.shape[0]
    capacity = 2 * observed // bands
    slots = capacity * bands
    group = nodes // bands
    blocks = block_mask.shape[1]
    tiles = nodes // TILE
    passes = heads // HEADS_PER_PASS
    low, wide = jnp.bfloat16, jnp.float32
    dma = pltpu.SemaphoreType.DMA
    vmem = pl.BlockSpec(memory_space=pltpu.VMEM)
    far = pl.BlockSpec(memory_space=pl.ANY)
    grads = pl.pallas_call(
        functools.partial(encoder_kernel, bands, models),
        out_shape=(
            jax.ShapeDtypeStruct((nodes, columns), low),
            jax.ShapeDtypeStruct((observed, columns), low),
        ),
        in_specs=[far, vmem, far, far, vmem, vmem, vmem, far, far, far, far],
        out_specs=(vmem, vmem),
        scratch_shapes=[
            pltpu.VMEM(node_adjoint.shape, low),
            pltpu.VMEM(latents.shape, low),
            pltpu.VMEM(observations.shape, low),
            pltpu.VMEM(w_query.shape, low),
            pltpu.VMEM(w_key.shape, low),
            pltpu.VMEM(w_value.shape, low),
            pltpu.VMEM(w_out.shape, low),
            dma((7,)),
            pltpu.VMEM((bands, capacity, columns), low),
            pltpu.VMEM((bands, 16, capacity), low),
            pltpu.VMEM((bands, group, columns), low),
            pltpu.VMEM((models, bands, capacity, columns), low),
            pltpu.VMEM((bands, 16, capacity), low),
            pltpu.VMEM((bands, group, columns), low),
            pltpu.VMEM((bands, group, columns), low),
            pltpu.VMEM((nodes, columns), low),
            pltpu.VMEM((tiles, columns, TILE), low),
            pltpu.VMEM((nodes, columns), low),
            pltpu.VMEM((nodes, columns), low),
            pltpu.VMEM((nodes, columns), low),
            pltpu.VMEM((tiles, columns, TILE), low),
            pltpu.VMEM((heads, slots, columns), low),
            pltpu.VMEM((heads, slots, columns), low),
            pltpu.VMEM((blocks, 1, slots), wide),
            pltpu.VMEM((columns, slots), wide),
            pltpu.VMEM((columns, slots), wide),
            pltpu.VMEM((heads, nodes, slots), low),
            pltpu.VMEM((nodes, columns), wide),
            pltpu.VMEM((nodes, columns), wide),
            pltpu.VMEM((nodes, nodes), low),
            pltpu.VMEM((observed, slots), low),
            pltpu.VMEM((nodes, columns), wide),
            pltpu.VMEM((bands, 2 * columns, capacity), low),
            pltpu.VMEM((bands, 2 * columns, capacity), low),
            pltpu.VMEM((2, tiles, chips, TILE, columns), low),
            pltpu.VMEM((tiles, chips, TILE, columns), low),
            pltpu.VMEM((chips - 1, tiles, TILE, columns), low),
            pltpu.VMEM((chips - 1, tiles, TILE, columns), low),
            pltpu.VMEM((2, chips, observed, columns), low),
            pltpu.VMEM((chips, observed, columns), low),
            pltpu.VMEM((chips - 1, observed, columns), low),
            pltpu.VMEM((chips - 1, observed, columns), low),
            dma((4, bands)),
            dma((4, bands)),
            dma((models - 1, bands)),
            dma((models - 1, bands)),
            dma((2 * passes, bands)),
            dma((2 * passes, bands)),
            dma((chips - 1, tiles + 1)),
            dma((chips - 1, tiles + 1)),
            dma((tiles + 1,)),
            dma((tiles + 1,)),
        ],
        compiler_params=pltpu.CompilerParams(collective_id=0, has_side_effects=True),
    )(
        node_adjoint,
        band_map,
        latents,
        observations,
        route_band.reshape(1, observed),
        route_cell.reshape(1, observed),
        block_mask,
        w_query,
        w_key,
        w_value,
        w_out,
    )
    return pl.pallas_call(
        write_kernel,
        out_shape=tuple(jax.ShapeDtypeStruct(g.shape, g.dtype) for g in grads),
        in_specs=(vmem, vmem),
        out_specs=(vmem, vmem),
    )(*grads)


def solution(mesh):
    bands = mesh.shape["band"]

    def body(*arrays):
        capacity = 2 * arrays[3].shape[0] // bands
        group = arrays[0].shape[0] // bands
        tiled = capacity % 128 == 0 and group % 16 == 0
        return (on_device if tiled else on_device_plain)(*arrays)

    return jax.shard_map(
        body,
        mesh=mesh,
        in_specs=(
            P("band", None),
            P("band", None),
            P("band", None),
            P("band", None),
            P("band", None),
            P("band"),
            P("band", None),
            P(None, "mp"),
            P(None, "mp"),
            P(None, "mp"),
            P("mp", None),
        ),
        out_specs=(P("band", "mp"), P("band", "mp")),
        check_vma=False,
    )
```
